512 devices in a mesh: region: 8 (over x, z_hi), dev: 64 (over y, z_lo, core).
Axes of the slice: x: 4, y: 8, z: 8 (z_hi: 2, z_lo: 4; z = z_hi * 4 + z_lo), core: 2. Of those that a mesh axis runs over, the one named last changes fastest.
Arguments:
- object_field: float32 [2, 131072, 512], P(None, ('region', 'dev')), may hold values from -6 to 6
- probe: float32 [2, 256, 256], replicated, may hold values from -6 to 6
- amplitudes: float32 [8, 64, 4, 256, 256], P('region', 'dev'), may hold values from 0.5 to 4
- row_offset: int32 [8, 64, 4], P('region', 'dev'), may hold values from 0 to 255
- col_offset: int32 [8, 64, 4], P('region', 'dev'), may hold values from 0 to 256
- frame_count: int32 [8, 64], P('region', 'dev'), may hold values from 1 to 4, as said below
Outputs:
- new_object: float32 [2, 131072, 512], P(None, ('region', 'dev'))
- new_probe: float32 [2, 256, 256], replicated
The draws below stay inside these ranges and needn't reach their ends.
Inputs may be any that keep to these rules, and one draw needn't show every extreme that they name: `frame_count`: in each region, device j and device j + 32 together hold at most 6 frames, and some device holds 4.
All inputs are finite; a program needn't handle non-finite values.
Results may differ from the reference program's by a relative error of at most 0.0003.
Values sent between devices are 32-bit elements; how exact they have to be, the bound alone decides.
No kernel may reach another device: no remote copies, remote signals or barrier semaphores. Data moves between devices by JAX's collectives and lax.ppermute only.
A program may use at most 64 MiB of HBM per device.

```python
import jax
import jax.numpy as jnp
from jax import lax

FRAME = 256
BAND = 256
WIDTH = 512
FRAMES_DEV = 4
ITERS = 1
REGIONS = 8
DEVS = 64
ROWS = 131072
N_REGION = 8
N_DEV = 64


def draw_frame_count(key, part):
    half_devs = DEVS // 2
    streams = jax.random.split(jax.random.fold_in(key, 11), 4)
    heavy = jax.random.randint(streams[0], (REGIONS, half_devs), FRAMES_DEV // 2, FRAMES_DEV + 1)
    forced = jax.random.randint(streams[1], (REGIONS, 1), 0, half_devs)
    heavy = jnp.where(jnp.arange(half_devs)[None, :] == forced, FRAMES_DEV, heavy)
    ceiling = jnp.minimum(FRAMES_DEV, FRAMES_DEV + FRAMES_DEV // 2 - heavy)
    light = jax.random.randint(streams[2], (REGIONS, half_devs), 1, ceiling + 1)
    flips = jax.random.randint(streams[3], (REGIONS, half_devs), 0, 2)
    first_half = jnp.where(flips == 1, heavy, light)
    second_half = jnp.where(flips == 1, light, heavy)
    return jnp.concatenate([first_half, second_half], axis=1).astype(jnp.int32)


def place_ends(drawn, stream_key, smallest, high):
    shape = drawn.shape
    place = [jax.random.randint(jax.random.fold_in(stream_key, axis), (), 0, shape[axis]) for axis in range(len(shape))]
    drawn = drawn.at[tuple(place)].set(smallest)
    longest = shape.index(max(shape))
    place[longest] = (place[longest] + 1) % shape[longest]
    return drawn.at[tuple(place)].set(high)


def shard_levels(own_key, dims, cuts, least, high):
    gain, own = 1.0, jax.random.fold_in(own_key, 6)
    for axis_at, parts in cuts:
        steps = jnp.exp(jax.random.uniform(jax.random.fold_in(own, axis_at), (parts,), jnp.float32, least / len(cuts), high / len(cuts)))
        gain = gain * jnp.repeat(steps, dims[axis_at] // parts).reshape([-1 if axis == axis_at else 1 for axis in range(len(dims))])
    return gain


def bell_draw(key, shape, width, bound, shards=(), held_as=jnp.bfloat16):
    array = width * jax.random.normal(key, shape, jnp.float32)
    if shards:
        array = array * shard_levels(key, shape, shards, -0.22, 0.18)
    return jnp.clip(array, -bound, bound).astype(held_as)


def setup_inputs(seed: int = 0) -> dict:
    keys = jax.random.split(jax.random.key(seed), 7)
    object_field = bell_draw(keys[0], (2, ROWS, WIDTH), 1.0, 6.0, ((1, 512),), jnp.float32)
    probe = bell_draw(keys[1], (2, FRAME, FRAME), 1.0, 6.0, (), jnp.float32)
    amplitudes = jnp.clip(0.5 + 3.5 * jax.random.uniform(keys[2], (REGIONS, DEVS, FRAMES_DEV, FRAME, FRAME), jnp.float32) ** shard_levels(keys[2], (REGIONS, DEVS, FRAMES_DEV, FRAME, FRAME), ((0, 8), (1, 64)), -0.2, 0.2), 0.5, 4.0)
    row_offset = place_ends(jax.random.randint(keys[3], (REGIONS, DEVS, FRAMES_DEV), 0, BAND), jax.random.fold_in(keys[3], 1), 0, BAND - 1).astype(jnp.int32)
    col_offset = place_ends(jax.random.randint(keys[4], (REGIONS, DEVS, FRAMES_DEV), 0, WIDTH - FRAME + 1), jax.random.fold_in(keys[4], 1), 0, WIDTH - FRAME).astype(jnp.int32)
    frame_count = draw_frame_count(jax.random.fold_in(keys[6], 71), 0)
    return {"object_field": object_field, "probe": probe, "amplitudes": amplitudes, "row_offset": row_offset, "col_offset": col_offset, "frame_count": frame_count}


def fourier_wave(windows, probe, measured, live_mask):
    object_wave = windows[:, 0] + 1j * windows[:, 1]
    probe_wave = probe[0] + 1j * probe[1]
    spectrum = jnp.fft.fft2(probe_wave[None] * object_wave, norm='ortho')
    modulus = jnp.sqrt(jnp.real(spectrum) ** 2 + jnp.imag(spectrum) ** 2 + 0.25)
    corrected = spectrum * (1.0 - measured / modulus)
    returned = jnp.fft.ifft2(corrected, norm='ortho') * live_mask[:, None, None]
    return (jnp.real(returned), jnp.imag(returned))

def region_pass(region_object, probe, measured, row_starts, col_starts, live_mask):
    span_rows = region_object.shape[1]
    padded = jnp.pad(region_object, ((0, 0), (0, FRAME), (0, 0)))

    def window_cut(row_start, col_start):
        return lax.dynamic_slice(padded, (jnp.int32(0), row_start.astype(jnp.int32), col_start.astype(jnp.int32)), (2, FRAME, FRAME))
    windows = jax.vmap(window_cut)(row_starts, col_starts)
    back_real, back_imag = fourier_wave(windows, probe, measured, live_mask)
    grad_real = lax.optimization_barrier(jnp.sum(windows[:, 0] * back_real + windows[:, 1] * back_imag, axis=0))
    grad_imag = lax.optimization_barrier(jnp.sum(windows[:, 0] * back_imag - windows[:, 1] * back_real, axis=0))
    power = probe[0] * probe[0] + probe[1] * probe[1]
    pieces = jnp.stack([probe[0] * back_real + probe[1] * back_imag, probe[0] * back_imag - probe[1] * back_real, power[None] * live_mask[:, None, None]], axis=1)

    def accumulate(index, totals):
        row_start = row_starts[index].astype(jnp.int32)
        col_start = col_starts[index].astype(jnp.int32)
        anchor = (jnp.int32(0), row_start, col_start)
        current = lax.dynamic_slice(totals, anchor, (3, FRAME, FRAME))
        return lax.dynamic_update_slice(totals, current + pieces[index], anchor)
    totals = lax.fori_loop(0, pieces.shape[0], accumulate, jnp.zeros((3, span_rows + FRAME, region_object.shape[2]), jnp.float32))
    updated = region_object - totals[:2, :span_rows] / (totals[2:3, :span_rows] + 1.0)
    return (updated, jnp.stack([grad_real, grad_imag]))

def reference(object_field, probe, amplitudes, row_offset, col_offset, frame_count):
    span_rows = N_DEV * BAND
    regions = object_field.reshape(2, N_REGION, span_rows, WIDTH).transpose(1, 0, 2, 3)
    band_starts = (jnp.arange(N_DEV, dtype=jnp.int32) * BAND)[None, :, None]
    row_starts = (row_offset + band_starts).astype(jnp.int32).reshape(N_REGION, -1)
    col_starts = col_offset.astype(jnp.int32).reshape(N_REGION, -1)
    slot_index = jnp.arange(FRAMES_DEV, dtype=jnp.int32)[None, None, :]
    live_mask = (slot_index < frame_count[:, :, None]).astype(jnp.float32).reshape(N_REGION, -1)
    measured = amplitudes.reshape(N_REGION, -1, FRAME, FRAME)
    for iteration in range(ITERS):
        current_probe = probe

        def one_region(inputs):
            return region_pass(inputs[0], current_probe, inputs[1], inputs[2], inputs[3], inputs[4])
        regions, gradients = lax.map(one_region, (regions, measured, row_starts, col_starts, live_mask))
        summed = lax.optimization_barrier(jnp.sum(gradients, axis=0))
        spread = jnp.sqrt(jnp.mean(summed * summed) + 1e-06)
        probe = probe - 0.25 * summed / spread
    new_object = regions.transpose(1, 0, 2, 3).reshape(2, N_REGION * span_rows, WIDTH)
    return (new_object, probe)
```

```python
import numpy as np
import ml_dtypes

import jax
import jax.numpy as jnp
from jax import lax
from jax.experimental import pallas as pl
from jax.experimental.pallas import tpu as pltpu
from jax.sharding import PartitionSpec as P

AXES = ("region", "dev")
BLOCK = 32


def in_two(table):
    high = table.astype(ml_dtypes.bfloat16)
    low = (table - high.astype(np.float64)).astype(ml_dtypes.bfloat16)
    return high, low


def half_tables(length):
    half = length // 2
    k = np.arange(half)[:, None]
    n = np.arange(half)[None, :]
    forms = []
    for shift in (0, 1):
        turn = (n * (2 * k + shift)) % length
        angle = -2.0 * np.pi * turn / length
        real = np.cos(angle) / np.sqrt(length)
        imag = np.sin(angle) / np.sqrt(length)
        forms.append(np.block([[real, -imag], [imag, real]]))
    return forms


def frame_tables(length):
    left, right = [], []
    for form in half_tables(length):
        high, low = in_two(form)
        left.append(np.concatenate([high, high, low], axis=1))
        high_t, low_t = high.T, low.T
        right.append(np.concatenate([high_t, high_t, low_t], axis=1))
    lefts = np.stack([left[0], left[1], right[0], right[1]])
    downs = []
    for form in half_tables(length):
        high, low = in_two(form)
        downs.append((np.concatenate([high.T, high.T, low.T], axis=0), np.concatenate([high, high, low], axis=0)))
    rights = np.stack([downs[0][0], downs[1][0], downs[0][1], downs[1][1]])
    return lefts, rights


def order_table(length):
    half = length // 2
    table = np.zeros((length, length), np.float32)
    table[2 * np.arange(half), np.arange(half)] = 1.0
    table[2 * np.arange(half) + 1, half + np.arange(half)] = 1.0
    return table.astype(ml_dtypes.bfloat16)


def split2(x):
    high = x.astype(jnp.bfloat16)
    low = (x - high.astype(jnp.float32)).astype(jnp.bfloat16)
    return high, low


def placed(row, col):
    block = jnp.minimum(col // 128, 1)
    return (
        pl.multiple_of(row // 8 * 8, 8),
        row % 8,
        pl.multiple_of(block * 128, 128),
        col - block * 128,
    )


def tiles(x):
    return x.reshape(x.shape[0] // 8, 8, x.shape[1])


def cut_columns(x, rest):
    shift = (128 - rest) & 127
    r = [pltpu.roll(x[:, 128 * j : 128 * j + 128], shift, axis=1) for j in range(3)]
    inside = lax.broadcasted_iota(jnp.int32, r[0].shape, 1) < 128 - rest
    return jnp.concatenate([jnp.where(inside, r[0], r[1]), jnp.where(inside, r[1], r[2])], axis=1)


def turned(x, shift):
    return pltpu.roll(tiles(x), shift & 7, axis=1)


def read_window(read, size, rest_row, rest_col, use):
    after = turned(cut_columns(read(size, 8), rest_col), 8 - rest_row)
    for i in reversed(range(size // BLOCK)):
        here = turned(cut_columns(read(i * BLOCK, BLOCK), rest_col), 8 - rest_row)
        later = jnp.concatenate([here[1:], after], axis=0)
        sub = lax.broadcasted_iota(jnp.int32, here.shape, 1)
        use(i, jnp.where(sub < 8 - rest_row, here, later).reshape(BLOCK, -1))
        after = here[:1]


def moved_columns(x, rest):
    shift = rest & 127
    ra = pltpu.roll(x[:, :128], shift, axis=1)
    rb = pltpu.roll(x[:, 128:], shift, axis=1)
    inside = lax.broadcasted_iota(jnp.int32, ra.shape, 1) >= rest
    zero = jnp.zeros_like(ra)
    return jnp.concatenate(
        [jnp.where(inside, ra, zero), jnp.where(inside, rb, ra), jnp.where(inside, zero, rb)], axis=1
    )


def moved_rows(x, before, rest_row):
    here = turned(x, rest_row)
    earlier = jnp.concatenate([before, here[:-1]], axis=0)
    sub = lax.broadcasted_iota(jnp.int32, here.shape, 1)
    return jnp.where(sub >= rest_row, here, earlier).reshape(x.shape), here[-1:]


def last_rows(before, rest_row):
    sub = lax.broadcasted_iota(jnp.int32, before.shape, 1)
    return jnp.where(sub >= rest_row, 0.0, before).reshape(8, -1)


def prepare_kernel(rows, cols, counts, amp_ref, probe_ref, order_ref, out_ref, weight_ref, total, side):
    band = weight_ref.shape[0]
    size = probe_ref.shape[1]
    half = size // 2
    total[...] = jnp.zeros_like(total)

    def add_power(source, frame, down):
        start, rest_row, base, rest_col = placed(rows[source, frame], cols[source, frame])
        before = jnp.zeros((1, 8, 384), jnp.float32)
        for i in range(size // BLOCK):
            pr = probe_ref[0, i * BLOCK : (i + 1) * BLOCK, :]
            pi = probe_ref[1, i * BLOCK : (i + 1) * BLOCK, :]
            part, before = moved_rows(moved_columns(pr * pr + pi * pi, rest_col), before, rest_row)
            place = (pl.ds(start + (down + i * BLOCK), BLOCK), pl.ds(base, 384))
            total[place] = total[place] + part
        place = (pl.ds(start + (down + size), 8), pl.ds(base, 384))
        total[place] = total[place] + last_rows(before, rest_row)

    def own(frame, carry):
        add_power(0, frame, band)
        return carry

    def previous(frame, carry):
        add_power(1, frame, 0)
        return carry

    lax.fori_loop(0, counts[0], own, 0)
    lax.fori_loop(0, counts[1], previous, 0)
    for i in range(band // BLOCK):
        weight_ref[i * BLOCK : (i + 1) * BLOCK, :] = 1.0 / (
            total[band + i * BLOCK : band + (i + 1) * BLOCK, :] + 1.0
        )

    def permute(frame, carry):
        x = amp_ref[frame]
        high = x.astype(jnp.bfloat16)
        left = x - high.astype(jnp.float32)
        mid = left.astype(jnp.bfloat16)
        low = (left - mid.astype(jnp.float32)).astype(jnp.bfloat16)
        order = order_ref[...]
        y = (
            jnp.dot(high, order, preferred_element_type=jnp.float32)
            + jnp.dot(mid, order, preferred_element_type=jnp.float32)
            + jnp.dot(low, order, preferred_element_type=jnp.float32)
        )
        for j in (0, 1):
            column = slice(j * half, (j + 1) * half)
            side[...] = y[:, column]
            for parity in (0, 1):
                out_ref[frame, parity * half : (parity + 1) * half, column] = side[
                    pl.ds(parity, half, stride=2), :
                ]
        return carry

    lax.fori_loop(0, counts[0], permute, 0)


def frames_kernel(
    rows, cols, counts, field_ref, rim_ref, probe_ref, amp_ref, lefts, rights,
    mine_ref, other_ref, own_ref, over_ref,
    ext, win, xh, xl, fa, fb, total, grad,
):
    band = field_ref.shape[1]
    size = probe_ref.shape[1]
    half = size // 2
    steps = half // BLOCK
    ext[:, :band] = field_ref[...]
    ext[:, band:] = rim_ref[...]
    total[...] = jnp.zeros_like(total)
    grad[...] = jnp.zeros_like(grad)

    def keep(which, place, value):
        high, low = split2(value)
        xh[(which, *place)] = high
        xl[(which, *place)] = low

    def by_right(which, table):
        high = xh[which]
        x = jnp.concatenate([high, xl[which], high], axis=1)
        return jnp.dot(x, rights[table], preferred_element_type=jnp.float32)

    def by_left(which, table):
        high = xh[which]
        x = jnp.concatenate([high, xl[which], high], axis=0)
        return jnp.dot(lefts[table], x, preferred_element_type=jnp.float32)

    def one_frame(frame, carry):
        start, rest_row, base, rest_col = placed(rows[0, frame], cols[0, frame])

        def into(c):
            def use(i, rows_cut):
                win[c, i * BLOCK : (i + 1) * BLOCK, :] = rows_cut

            return use

        for c in (0, 1):
            read_window(
                lambda at, count: ext[c, pl.ds(start + at, count), pl.ds(base, 384)],
                size, rest_row, rest_col, into(c),
            )
        for i in range(size // BLOCK):
            row = slice(i * BLOCK, (i + 1) * BLOCK)
            wr, wi = win[0, row, :], win[1, row, :]
            pr, pi = probe_ref[0, row, :], probe_ref[1, row, :]
            er = pr * wr - pi * wi
            ei = pr * wi + pi * wr
            keep(0, (row, slice(0, half)), er[:, :half] + er[:, half:])
            keep(0, (row, slice(half, size)), ei[:, :half] + ei[:, half:])
            keep(1, (row, slice(0, half)), er[:, :half] - er[:, half:])
            keep(1, (row, slice(half, size)), ei[:, :half] - ei[:, half:])
        fa[...] = by_right(0, 0)
        fb[...] = by_right(1, 1)
        for i in range(steps):
            top = slice(i * BLOCK, (i + 1) * BLOCK)
            low = slice(half + i * BLOCK, half + (i + 1) * BLOCK)
            for ref, out in ((fa, slice(0, half)), (fb, slice(half, size))):
                t, b = ref[top, :], ref[low, :]
                s, d = t + b, t - b
                keep(0, (top, out), s[:, :half])
                keep(0, (low, out), s[:, half:])
                keep(1, (top, out), d[:, :half])
                keep(1, (low, out), d[:, half:])
        fa[...] = by_left(0, 0)
        fb[...] = by_left(1, 1)
        for i in range(steps):
            top = slice(i * BLOCK, (i + 1) * BLOCK)
            low = slice(half + i * BLOCK, half + (i + 1) * BLOCK)
            for which, ref in ((0, fa), (1, fb)):
                re, im = ref[top, :], ref[low, :]
                a = amp_ref[frame, pl.ds(which * half + i * BLOCK, BLOCK), :]
                factor = 1.0 - a * lax.rsqrt(re * re + im * im + 0.25)
                keep(which, (top, slice(0, size)), re * factor)
                keep(which, (low, slice(0, size)), im * factor)
        fa[...] = by_left(0, 2)
        fb[...] = by_left(1, 3)
        for i in range(steps):
            top = slice(i * BLOCK, (i + 1) * BLOCK)
            low = slice(half + i * BLOCK, half + (i + 1) * BLOCK)
            for part, out in ((top, slice(0, half)), (low, slice(half, size))):
                p, q = fa[part, :], fb[part, :]
                s, d = p + q, p - q
                for place, v in ((top, s), (low, d)):
                    keep(0, (place, out), v[:, :half])
                    keep(1, (place, out), v[:, half:])
        fa[...] = by_right(0, 2)
        fb[...] = by_right(1, 3)
        before = [jnp.zeros((1, 8, 384), jnp.float32)] * 2
        for i in range(size // BLOCK):
            row = slice(i * BLOCK, (i + 1) * BLOCK)
            p, q = fa[row, :], fb[row, :]
            s, d = p + q, p - q
            br = jnp.concatenate([s[:, :half], d[:, :half]], axis=1)
            bi = jnp.concatenate([s[:, half:], d[:, half:]], axis=1)
            wr, wi = win[0, row, :], win[1, row, :]
            grad[0, row, :] = grad[0, row, :] + (wr * br + wi * bi)
            grad[1, row, :] = grad[1, row, :] + (wr * bi - wi * br)
            pr, pi = probe_ref[0, row, :], probe_ref[1, row, :]
            for c, v in ((0, pr * br + pi * bi), (1, pr * bi - pi * br)):
                part, before[c] = moved_rows(moved_columns(v, rest_col), before[c], rest_row)
                place = (c, pl.ds(start + i * BLOCK, BLOCK), pl.ds(base, 384))
                total[place] = total[place] + part
        for c in (0, 1):
            place = (c, pl.ds(start + size, 8), pl.ds(base, 384))
            total[place] = total[place] + last_rows(before[c], rest_row)
        return carry

    lax.fori_loop(0, counts[0], one_frame, 0)
    own_ref[...] = total[:, :band]
    over_ref[...] = total[:, band:]
    first = counts[2] == 0
    for i in range(size // BLOCK):
        row = slice(i * BLOCK, (i + 1) * BLOCK)
        re, im = grad[0, row, :], grad[1, row, :]
        mine_ref[row, :] = jnp.where(first, re, im)
        other_ref[row, :] = jnp.where(first, im, re)


def place_of(device):
    region, dev = divmod(device, 64)
    return {
        "x": region // 2,
        "z": (region % 2) * 4 + (dev // 2) % 4,
        "y": dev // 8,
        "core": dev % 2,
    }


def groups_along(names):
    groups = {}
    for device in range(512):
        place = place_of(device)
        key = tuple(v for k, v in place.items() if k not in names)
        groups.setdefault(key, []).append(device)
    return list(groups.values())


def exchanged(parts, names):
    return lax.all_to_all(parts, AXES, 0, 0, tiled=True, axis_index_groups=groups_along(names))


def copies(part, names):
    peers = len(groups_along(names)[0])
    return exchanged(jnp.broadcast_to(part[None], (peers, *part.shape)), names)


def on_device(object_field, probe, amplitudes, row_offset, col_offset, frame_count):
    band, width = object_field.shape[1:]
    size = probe.shape[1]
    slots = amplitudes.shape[2]
    smem = pl.BlockSpec(memory_space=pltpu.SMEM)
    vmem = pl.BlockSpec(memory_space=pltpu.VMEM)
    f32 = jnp.float32
    peers = lax.axis_size("dev")

    rim = lax.ppermute(object_field, "dev", [(i, i - 1) for i in range(1, peers)])
    facts = jnp.concatenate([row_offset[0, 0], col_offset[0, 0], frame_count[0]])
    facts_before = lax.ppermute(facts, "dev", [(i, i + 1) for i in range(peers - 1)])
    both = jnp.stack([facts, facts_before])
    rows, cols = both[:, :slots], both[:, slots : 2 * slots]
    core = lax.axis_index("dev") % 2
    counts = jnp.concatenate([both[:, 2 * slots], core[None]])

    lefts, rights = frame_tables(size)
    ordered, scale = pl.pallas_call(
        prepare_kernel,
        out_shape=(
            jax.ShapeDtypeStruct((slots, size, size), f32),
            jax.ShapeDtypeStruct((band, width), f32),
        ),
        in_specs=[smem, smem, smem, vmem, vmem, vmem],
        out_specs=(vmem, vmem),
        scratch_shapes=[
            pltpu.VMEM((2 * band + size, width), f32),
            pltpu.VMEM((size, size // 2), f32),
        ],
        cost_estimate=pl.CostEstimate(flops=800_000_000, bytes_accessed=3_200_000, transcendentals=0),
        name="prepare",
    )(rows, cols, counts, amplitudes[0, 0], probe, jnp.asarray(order_table(size)))

    bf16 = jnp.bfloat16
    mine, other, own, over = pl.pallas_call(
        frames_kernel,
        out_shape=(
            jax.ShapeDtypeStruct((size, size), f32),
            jax.ShapeDtypeStruct((size, size), f32),
            jax.ShapeDtypeStruct((2, band, width), f32),
            jax.ShapeDtypeStruct((2, size, width), f32),
        ),
        in_specs=[smem, smem, smem, vmem, vmem, vmem, vmem, vmem, vmem],
        out_specs=(vmem, vmem, vmem, vmem),
        scratch_shapes=[
            pltpu.VMEM((2, band + size, width), f32),
            pltpu.VMEM((2, size, size), f32),
            pltpu.VMEM((2, size, size), bf16),
            pltpu.VMEM((2, size, size), bf16),
            pltpu.VMEM((size, size), f32),
            pltpu.VMEM((size, size), f32),
            pltpu.VMEM((2, band + size, width), f32),
            pltpu.VMEM((2, size, size), f32),
        ],
        compiler_params=pltpu.CompilerParams(vmem_limit_bytes=40 * 1024 * 1024),
        cost_estimate=pl.CostEstimate(flops=3_300_000_000, bytes_accessed=8_000_000, transcendentals=262144),
        name="frames",
    )(rows, cols, counts, object_field, rim, probe, ordered, jnp.asarray(lefts), jnp.asarray(rights))

    swap = [(i, i ^ 1) for i in range(peers)]
    plane = mine + lax.ppermute(other, "dev", swap)
    parts = exchanged(plane.reshape(32, size // 32, size), ("x", "z"))
    share = jnp.sum(parts, axis=0)
    share = jnp.sum(copies(share, ("y",)), axis=0)
    plane = copies(share, ("x", "z")).reshape(size, size)
    plane_other = lax.ppermute(plane, "dev", swap)

    incoming = lax.ppermute(over, "dev", [(i, i + 1) for i in range(peers - 1)])
    new_field = object_field - jnp.concatenate(
        [own[:, :size] + incoming, own[:, size:]], axis=1
    ) * scale[None]

    squares = jnp.sum(plane * plane + plane_other * plane_other)
    step = 0.25 * lax.rsqrt(squares / (2 * size * size) + 1e-06)
    real = jnp.where(core == 0, plane, plane_other)
    imag = jnp.where(core == 0, plane_other, plane)
    new_probe = jnp.stack([probe[0] - step * real, probe[1] - step * imag])
    return (new_field, new_probe)


def solution(mesh):
    return jax.shard_map(
        on_device,
        mesh=mesh,
        in_specs=(
            P(None, ("region", "dev"), None),
            P(),
            P("region", "dev", None, None, None),
            P("region", "dev", None),
            P("region", "dev", None),
            P("region", "dev"),
        ),
        out_specs=(P(None, ("region", "dev"), None), P()),
        check_vma=False,
    )
```

```python
import numpy as np
import ml_dtypes

import jax
import jax.numpy as jnp
from jax import lax
from jax.experimental import pallas as pl
from jax.experimental.pallas import tpu as pltpu
from jax.sharding import PartitionSpec as P

AXES = ("region", "dev")
BLOCK = 32
WIDE = (("x", "z"), ("x", "y"))
LINE = (("y",), ("z",))


def in_two(table):
    high = table.astype(ml_dtypes.bfloat16)
    low = (table - high.astype(np.float64)).astype(ml_dtypes.bfloat16)
    return high, low


def half_tables(length):
    half = length // 2
    k = np.arange(half)[:, None]
    n = np.arange(half)[None, :]
    forms = []
    for shift in (0, 1):
        turn = (n * (2 * k + shift)) % length
        angle = -2.0 * np.pi * turn / length
        real = np.cos(angle) / np.sqrt(length)
        imag = np.sin(angle) / np.sqrt(length)
        forms.append(np.block([[real, -imag], [imag, real]]))
    return forms


def frame_tables(length):
    first, second = half_tables(length)
    parts = [in_two(form) for form in (first, first.T, second, second.T)]
    return np.stack([np.stack(pair) for pair in parts])


def order_table(length):
    half = length // 2
    table = np.zeros((length, length), np.float32)
    table[2 * np.arange(half), np.arange(half)] = 1.0
    table[2 * np.arange(half) + 1, half + np.arange(half)] = 1.0
    return table.astype(ml_dtypes.bfloat16)


def split2(x):
    high = x.astype(jnp.bfloat16)
    low = (x - high.astype(jnp.float32)).astype(jnp.bfloat16)
    return high, low


def placed(row, col):
    block = jnp.minimum(col // 128, 1)
    return (
        pl.multiple_of(row // 8 * 8, 8),
        row % 8,
        pl.multiple_of(block * 128, 128),
        col - block * 128,
    )


def tiles(x):
    return x.reshape(x.shape[0] // 8, 8, x.shape[1])


def cut_columns(x, rest):
    shift = (128 - rest) & 127
    r = [pltpu.roll(x[:, 128 * j : 128 * j + 128], shift, axis=1) for j in range(3)]
    inside = lax.broadcasted_iota(jnp.int32, r[0].shape, 1) < 128 - rest
    return jnp.concatenate([jnp.where(inside, r[0], r[1]), jnp.where(inside, r[1], r[2])], axis=1)


def turned(x, shift):
    return pltpu.roll(tiles(x), shift & 7, axis=1)


def read_window(read, size, rest_row, rest_col, use):
    after = turned(cut_columns(read(size, 8), rest_col), 8 - rest_row)
    for i in reversed(range(size // BLOCK)):
        here = turned(cut_columns(read(i * BLOCK, BLOCK), rest_col), 8 - rest_row)
        later = jnp.concatenate([here[1:], after], axis=0)
        sub = lax.broadcasted_iota(jnp.int32, here.shape, 1)
        use(i, jnp.where(sub < 8 - rest_row, here, later).reshape(BLOCK, -1))
        after = here[:1]


def moved_columns(x, rest):
    shift = rest & 127
    ra = pltpu.roll(x[:, :128], shift, axis=1)
    rb = pltpu.roll(x[:, 128:], shift, axis=1)
    inside = lax.broadcasted_iota(jnp.int32, ra.shape, 1) >= rest
    zero = jnp.zeros_like(ra)
    return jnp.concatenate(
        [jnp.where(inside, ra, zero), jnp.where(inside, rb, ra), jnp.where(inside, zero, rb)], axis=1
    )


def moved_rows(x, before, rest_row):
    here = turned(x, rest_row)
    earlier = jnp.concatenate([before, here[:-1]], axis=0)
    sub = lax.broadcasted_iota(jnp.int32, here.shape, 1)
    return jnp.where(sub >= rest_row, here, earlier).reshape(x.shape), here[-1:]


def last_rows(before, rest_row):
    sub = lax.broadcasted_iota(jnp.int32, before.shape, 1)
    return jnp.where(sub >= rest_row, 0.0, before).reshape(8, -1)


def prepare_kernel(rows, cols, counts, amp_ref, probe_ref, order_ref, out_ref, weight_ref, total, side):
    band = weight_ref.shape[0]
    size = probe_ref.shape[1]
    half = size // 2
    total[...] = jnp.zeros_like(total)

    def add_power(source, frame, down):
        start, rest_row, base, rest_col = placed(rows[source, frame], cols[source, frame])
        before = jnp.zeros((1, 8, 384), jnp.float32)
        for i in range(size // BLOCK):
            pr = probe_ref[0, i * BLOCK : (i + 1) * BLOCK, :]
            pi = probe_ref[1, i * BLOCK : (i + 1) * BLOCK, :]
            part, before = moved_rows(moved_columns(pr * pr + pi * pi, rest_col), before, rest_row)
            place = (pl.ds(start + (down + i * BLOCK), BLOCK), pl.ds(base, 384))
            total[place] = total[place] + part
        place = (pl.ds(start + (down + size), 8), pl.ds(base, 384))
        total[place] = total[place] + last_rows(before, rest_row)

    def own(frame, carry):
        add_power(0, frame, band)
        return carry

    def previous(frame, carry):
        add_power(1, frame, 0)
        return carry

    lax.fori_loop(0, counts[0], own, 0)
    lax.fori_loop(0, counts[1], previous, 0)
    for i in range(band // BLOCK):
        weight_ref[i * BLOCK : (i + 1) * BLOCK, :] = 1.0 / (
            total[band + i * BLOCK : band + (i + 1) * BLOCK, :] + 1.0
        )

    def permute(frame, carry):
        x = amp_ref[frame]
        high = x.astype(jnp.bfloat16)
        left = x - high.astype(jnp.float32)
        mid = left.astype(jnp.bfloat16)
        low = (left - mid.astype(jnp.float32)).astype(jnp.bfloat16)
        order = order_ref[...]
        y = (
            jnp.dot(high, order, preferred_element_type=jnp.float32)
            + jnp.dot(mid, order, preferred_element_type=jnp.float32)
            + jnp.dot(low, order, preferred_element_type=jnp.float32)
        )
        for j in (0, 1):
            column = slice(j * half, (j + 1) * half)
            side[...] = y[:, column]
            for parity in (0, 1):
                out_ref[frame, parity * half : (parity + 1) * half, column] = side[
                    pl.ds(parity, half, stride=2), :
                ]
        return carry

    lax.fori_loop(0, counts[0], permute, 0)


def frames_kernel(
    rows, cols, counts, field_ref, rim_ref, probe_ref, amp_ref, tables_ref,
    mine_ref, other_ref, own_ref, over_ref,
    ext, amp, tables, win, xh, xl, fa, fb, total, grad, sems,
):
    band = field_ref.shape[1]
    size = probe_ref.shape[1]
    half = size // 2
    steps = half // BLOCK
    loads = [
        pltpu.make_async_copy(field_ref, ext.at[:, :band], sems.at[0]),
        pltpu.make_async_copy(rim_ref, ext.at[:, band:], sems.at[1]),
        pltpu.make_async_copy(tables_ref, tables, sems.at[2]),
        pltpu.make_async_copy(amp_ref, amp, sems.at[3]),
    ]
    for load in loads:
        load.start()
    total[...] = jnp.zeros_like(total)
    grad[...] = jnp.zeros_like(grad)
    for load in loads[:2]:
        load.wait()

    def keep(which, place, value):
        high, low = split2(value)
        xh[(which, *place)] = high
        xl[(which, *place)] = low

    def by_right(which, table):
        high = xh[which]
        x = jnp.concatenate([high, xl[which], high], axis=1)
        t = tables[table, 0]
        t = jnp.concatenate([t, t, tables[table, 1]], axis=0)
        return jnp.dot(x, t, preferred_element_type=jnp.float32)

    def by_left(which, table):
        high = xh[which]
        x = jnp.concatenate([high, xl[which], high], axis=0)
        t = tables[table, 0]
        t = jnp.concatenate([t, t, tables[table, 1]], axis=1)
        return jnp.dot(t, x, preferred_element_type=jnp.float32)

    def one_frame(frame, carry):
        start, rest_row, base, rest_col = placed(rows[0, frame], cols[0, frame])

        def into(c):
            def use(i, rows_cut):
                win[c, i * BLOCK : (i + 1) * BLOCK, :] = rows_cut

            return use

        for c in (0, 1):
            read_window(
                lambda at, count: ext[c, pl.ds(start + at, count), pl.ds(base, 384)],
                size, rest_row, rest_col, into(c),
            )
        for i in range(size // BLOCK):
            row = slice(i * BLOCK, (i + 1) * BLOCK)
            wr, wi = win[0, row, :], win[1, row, :]
            pr, pi = probe_ref[0, row, :], probe_ref[1, row, :]
            er = pr * wr - pi * wi
            ei = pr * wi + pi * wr
            keep(0, (row, slice(0, half)), er[:, :half] + er[:, half:])
            keep(0, (row, slice(half, size)), ei[:, :half] + ei[:, half:])
            keep(1, (row, slice(0, half)), er[:, :half] - er[:, half:])
            keep(1, (row, slice(half, size)), ei[:, :half] - ei[:, half:])

        @pl.when(frame == 0)
        def _():
            for load in loads[2:]:
                load.wait()

        fa[...] = by_right(0, 1)
        fb[...] = by_right(1, 3)
        for i in range(steps):
            top = slice(i * BLOCK, (i + 1) * BLOCK)
            low = slice(half + i * BLOCK, half + (i + 1) * BLOCK)
            for ref, out in ((fa, slice(0, half)), (fb, slice(half, size))):
                t, b = ref[top, :], ref[low, :]
                s, d = t + b, t - b
                keep(0, (top, out), s[:, :half])
                keep(0, (low, out), s[:, half:])
                keep(1, (top, out), d[:, :half])
                keep(1, (low, out), d[:, half:])
        fa[...] = by_left(0, 0)
        fb[...] = by_left(1, 2)
        for i in range(steps):
            top = slice(i * BLOCK, (i + 1) * BLOCK)
            low = slice(half + i * BLOCK, half + (i + 1) * BLOCK)
            for which, ref in ((0, fa), (1, fb)):
                re, im = ref[top, :], ref[low, :]
                a = amp[frame, pl.ds(which * half + i * BLOCK, BLOCK), :]
                factor = 1.0 - a * lax.rsqrt(re * re + im * im + 0.25)
                keep(which, (top, slice(0, size)), re * factor)
                keep(which, (low, slice(0, size)), im * factor)
        fa[...] = by_left(0, 1)
        fb[...] = by_left(1, 3)
        for i in range(steps):
            top = slice(i * BLOCK, (i + 1) * BLOCK)
            low = slice(half + i * BLOCK, half + (i + 1) * BLOCK)
            for part, out in ((top, slice(0, half)), (low, slice(half, size))):
                p, q = fa[part, :], fb[part, :]
                s, d = p + q, p - q
                for place, v in ((top, s), (low, d)):
                    keep(0, (place, out), v[:, :half])
                    keep(1, (place, out), v[:, half:])
        fa[...] = by_right(0, 0)
        fb[...] = by_right(1, 2)
        before = [jnp.zeros((1, 8, 384), jnp.float32)] * 2
        for i in range(size // BLOCK):
            row = slice(i * BLOCK, (i + 1) * BLOCK)
            p, q = fa[row, :], fb[row, :]
            s, d = p + q, p - q
            br = jnp.concatenate([s[:, :half], d[:, :half]], axis=1)
            bi = jnp.concatenate([s[:, half:], d[:, half:]], axis=1)
            wr, wi = win[0, row, :], win[1, row, :]
            grad[0, row, :] = grad[0, row, :] + (wr * br + wi * bi)
            grad[1, row, :] = grad[1, row, :] + (wr * bi - wi * br)
            pr, pi = probe_ref[0, row, :], probe_ref[1, row, :]
            for c, v in ((0, pr * br + pi * bi), (1, pr * bi - pi * br)):
                part, before[c] = moved_rows(moved_columns(v, rest_col), before[c], rest_row)
                place = (c, pl.ds(start + i * BLOCK, BLOCK), pl.ds(base, 384))
                total[place] = total[place] + part
        for c in (0, 1):
            place = (c, pl.ds(start + size, 8), pl.ds(base, 384))
            total[place] = total[place] + last_rows(before[c], rest_row)
        return carry

    lax.fori_loop(0, counts[0], one_frame, 0)
    stores = [
        pltpu.make_async_copy(total.at[:, band:], over_ref, sems.at[0]),
        pltpu.make_async_copy(total.at[:, :band], own_ref, sems.at[1]),
    ]
    for store in stores:
        store.start()
    first = counts[2] == 0
    for i in range(size // BLOCK):
        row = slice(i * BLOCK, (i + 1) * BLOCK)
        re, im = grad[0, row, :], grad[1, row, :]
        mine_ref[row, :] = jnp.where(first, re, im)
        other_ref[row, :] = jnp.where(first, im, re)
    for store in stores:
        store.wait()


def place_of(device):
    region, dev = divmod(device, 64)
    return {
        "x": region // 2,
        "z": (region % 2) * 4 + (dev // 2) % 4,
        "y": dev // 8,
        "core": dev % 2,
    }


def groups_along(by_core):
    groups = {}
    for device in range(512):
        place = place_of(device)
        key = tuple(v for k, v in place.items() if k not in by_core[place["core"]])
        groups.setdefault((place["core"], key), []).append(device)
    return list(groups.values())


def exchanged(parts, names):
    return lax.all_to_all(parts, AXES, 0, 0, tiled=True, axis_index_groups=groups_along(names))


def copies(part, names):
    peers = len(groups_along(names)[0])
    return exchanged(jnp.broadcast_to(part[None], (peers, *part.shape)), names)


def on_device(object_field, probe, amplitudes, row_offset, col_offset, frame_count):
    band, width = object_field.shape[1:]
    size = probe.shape[1]
    slots = amplitudes.shape[2]
    smem = pl.BlockSpec(memory_space=pltpu.SMEM)
    vmem = pl.BlockSpec(memory_space=pltpu.VMEM)
    hbm = pl.BlockSpec(memory_space=pltpu.HBM)
    f32 = jnp.float32
    peers = lax.axis_size("dev")

    rim = lax.ppermute(object_field, "dev", [(i, i - 1) for i in range(1, peers)])
    facts = jnp.concatenate([row_offset[0, 0], col_offset[0, 0], frame_count[0]])
    facts_before = lax.ppermute(facts, "dev", [(i, i + 1) for i in range(peers - 1)])
    both = jnp.stack([facts, facts_before])
    rows, cols = both[:, :slots], both[:, slots : 2 * slots]
    core = lax.axis_index("dev") % 2
    counts = jnp.concatenate([both[:, 2 * slots], core[None]])

    ordered, scale = pl.pallas_call(
        prepare_kernel,
        out_shape=(
            jax.ShapeDtypeStruct((slots, size, size), f32),
            jax.ShapeDtypeStruct((band, width), f32),
        ),
        in_specs=[smem, smem, smem, vmem, vmem, vmem],
        out_specs=(vmem, vmem),
        scratch_shapes=[
            pltpu.VMEM((2 * band + size, width), f32),
            pltpu.VMEM((size, size // 2), f32),
        ],
        compiler_params=pltpu.CompilerParams(vmem_limit_bytes=65000 * 1024),
        cost_estimate=pl.CostEstimate(flops=800_000_000, bytes_accessed=3_200_000, transcendentals=0),
        name="prepare",
    )(rows, cols, counts, amplitudes[0, 0], probe, jnp.asarray(order_table(size)))

    bf16 = jnp.bfloat16
    mine, other, own, over = pl.pallas_call(
        frames_kernel,
        out_shape=(
            jax.ShapeDtypeStruct((size, size), f32),
            jax.ShapeDtypeStruct((size, size), f32),
            jax.ShapeDtypeStruct((2, band, width), f32),
            jax.ShapeDtypeStruct((2, size, width), f32),
        ),
        in_specs=[smem, smem, smem, hbm, hbm, vmem, hbm, hbm],
        out_specs=(vmem, vmem, hbm, hbm),
        scratch_shapes=[
            pltpu.VMEM((2, band + size, width), f32),
            pltpu.VMEM((slots, size, size), f32),
            pltpu.VMEM((4, 2, size, size), bf16),
            pltpu.VMEM((2, size, size), f32),
            pltpu.VMEM((2, size, size), bf16),
            pltpu.VMEM((2, size, size), bf16),
            pltpu.VMEM((size, size), f32),
            pltpu.VMEM((size, size), f32),
            pltpu.VMEM((2, band + size, width), f32),
            pltpu.VMEM((2, size, size), f32),
            pltpu.SemaphoreType.DMA((4,)),
        ],
        compiler_params=pltpu.CompilerParams(vmem_limit_bytes=60 * 1024 * 1024),
        cost_estimate=pl.CostEstimate(flops=3_300_000_000, bytes_accessed=8_000_000, transcendentals=262144),
        name="frames",
    )(rows, cols, counts, object_field, rim, probe, ordered, jnp.asarray(frame_tables(size)))

    first = core == 0
    mine, other, first = lax.optimization_barrier((mine, other, first))
    swap = [(i, i ^ 1) for i in range(peers)]
    plane = mine + lax.ppermute(other, "dev", swap)
    parts = exchanged(plane.reshape(32, size // 32, size), WIDE)
    share = jnp.sum(parts, axis=0)
    share = jnp.sum(copies(share, LINE), axis=0)
    plane = copies(share, WIDE).reshape(size, size)
    plane_other = lax.ppermute(plane, "dev", swap)

    incoming = lax.ppermute(over, "dev", [(i, i + 1) for i in range(peers - 1)])
    new_field = object_field - jnp.concatenate(
        [own[:, :size] + incoming, own[:, size:]], axis=1
    ) * scale[None]

    squares = jnp.sum(plane * plane + plane_other * plane_other)
    step = 0.25 * lax.rsqrt(squares / (2 * size * size) + 1e-06)
    real = jnp.where(first, plane, plane_other)
    imag = jnp.where(first, plane_other, plane)
    new_probe = jnp.stack([probe[0] - step * real, probe[1] - step * imag])
    return (new_field, new_probe)


def solution(mesh):
    return jax.shard_map(
        on_device,
        mesh=mesh,
        in_specs=(
            P(None, ("region", "dev"), None),
            P(),
            P("region", "dev", None, None, None),
            P("region", "dev", None),
            P("region", "dev", None),
            P("region", "dev"),
        ),
        out_specs=(P(None, ("region", "dev"), None), P()),
        check_vma=False,
    )
```

```python
import numpy as np
import ml_dtypes

import jax
import jax.numpy as jnp
from jax import lax
from jax.experimental import pallas as pl
from jax.experimental.pallas import tpu as pltpu
from jax.sharding import PartitionSpec as P

AXES = ("region", "dev")
SLOTS = 4
COUNT, CORE = 2 * SLOTS, 2 * SLOTS + 1
BLOCK = 32
WIDE = (("x", "z"), ("x", "y"))
LINE = (("y",), ("z",))


def in_two(table):
    high = table.astype(ml_dtypes.bfloat16)
    low = (table - high.astype(np.float64)).astype(ml_dtypes.bfloat16)
    return high, low


def half_tables(length):
    half = length // 2
    k = np.arange(half)[:, None]
    n = np.arange(half)[None, :]
    forms = []
    for shift in (0, 1):
        turn = (n * (2 * k + shift)) % length
        angle = -2.0 * np.pi * turn / length
        real = np.cos(angle) / np.sqrt(length)
        imag = np.sin(angle) / np.sqrt(length)
        forms.append(np.block([[real, -imag], [imag, real]]))
    return forms


def frame_tables(length):
    first, second = half_tables(length)
    parts = [in_two(form) for form in (first, first.T, second, second.T)]
    return np.stack([np.stack(pair) for pair in parts])


def order_table(length):
    half = length // 2
    table = np.zeros((length, length), np.float32)
    table[2 * np.arange(half), np.arange(half)] = 1.0
    table[2 * np.arange(half) + 1, half + np.arange(half)] = 1.0
    return table.astype(ml_dtypes.bfloat16)


def split2(x):
    high = x.astype(jnp.bfloat16)
    low = (x - high.astype(jnp.float32)).astype(jnp.bfloat16)
    return high, low


def placed(row, col):
    block = jnp.minimum(col // 128, 1)
    return (
        pl.multiple_of(row // 8 * 8, 8),
        row % 8,
        pl.multiple_of(block * 128, 128),
        col - block * 128,
    )


def corner(facts, source, frame):
    return facts[source, frame], facts[source, SLOTS + frame]


def tiles(x):
    return x.reshape(x.shape[0] // 8, 8, x.shape[1])


def cut_columns(x, rest):
    shift = (128 - rest) & 127
    r = [pltpu.roll(x[:, 128 * j : 128 * j + 128], shift, axis=1) for j in range(3)]
    inside = lax.broadcasted_iota(jnp.int32, r[0].shape, 1) < 128 - rest
    return jnp.concatenate([jnp.where(inside, r[0], r[1]), jnp.where(inside, r[1], r[2])], axis=1)


def turned(x, shift):
    return pltpu.roll(tiles(x), shift & 7, axis=1)


def read_window(read, size, rest_row, rest_col, use):
    after = turned(cut_columns(read(size, 8), rest_col), 8 - rest_row)
    for i in reversed(range(size // BLOCK)):
        here = turned(cut_columns(read(i * BLOCK, BLOCK), rest_col), 8 - rest_row)
        later = jnp.concatenate([here[1:], after], axis=0)
        sub = lax.broadcasted_iota(jnp.int32, here.shape, 1)
        use(i, jnp.where(sub < 8 - rest_row, here, later).reshape(BLOCK, -1))
        after = here[:1]


def moved_columns(x, rest):
    shift = rest & 127
    ra = pltpu.roll(x[:, :128], shift, axis=1)
    rb = pltpu.roll(x[:, 128:], shift, axis=1)
    inside = lax.broadcasted_iota(jnp.int32, ra.shape, 1) >= rest
    zero = jnp.zeros_like(ra)
    return jnp.concatenate(
        [jnp.where(inside, ra, zero), jnp.where(inside, rb, ra), jnp.where(inside, zero, rb)], axis=1
    )


def moved_rows(x, before, rest_row):
    here = turned(x, rest_row)
    earlier = jnp.concatenate([before, here[:-1]], axis=0)
    sub = lax.broadcasted_iota(jnp.int32, here.shape, 1)
    return jnp.where(sub >= rest_row, here, earlier).reshape(x.shape), here[-1:]


def last_rows(before, rest_row):
    sub = lax.broadcasted_iota(jnp.int32, before.shape, 1)
    return jnp.where(sub >= rest_row, 0.0, before).reshape(8, -1)


def prepare_kernel(facts, amp_ref, probe_ref, order_ref, out_ref, weight_ref, total, side):
    band = weight_ref.shape[0]
    size = probe_ref.shape[1]
    half = size // 2
    total[...] = jnp.zeros_like(total)

    def add_power(source, frame, down):
        start, rest_row, base, rest_col = placed(*corner(facts, source, frame))
        before = jnp.zeros((1, 8, 384), jnp.float32)
        for i in range(size // BLOCK):
            pr = probe_ref[0, i * BLOCK : (i + 1) * BLOCK, :]
            pi = probe_ref[1, i * BLOCK : (i + 1) * BLOCK, :]
            part, before = moved_rows(moved_columns(pr * pr + pi * pi, rest_col), before, rest_row)
            place = (pl.ds(start + (down + i * BLOCK), BLOCK), pl.ds(base, 384))
            total[place] = total[place] + part
        place = (pl.ds(start + (down + size), 8), pl.ds(base, 384))
        total[place] = total[place] + last_rows(before, rest_row)

    def own(frame, carry):
        add_power(0, frame, band)
        return carry

    def previous(frame, carry):
        add_power(1, frame, 0)
        return carry

    lax.fori_loop(0, facts[0, COUNT], own, 0)
    lax.fori_loop(0, facts[1, COUNT], previous, 0)
    for i in range(band // BLOCK):
        weight_ref[i * BLOCK : (i + 1) * BLOCK, :] = 1.0 / (
            total[band + i * BLOCK : band + (i + 1) * BLOCK, :] + 1.0
        )

    def permute(frame, carry):
        x = amp_ref[frame]
        high = x.astype(jnp.bfloat16)
        left = x - high.astype(jnp.float32)
        mid = left.astype(jnp.bfloat16)
        low = (left - mid.astype(jnp.float32)).astype(jnp.bfloat16)
        order = order_ref[...]
        y = (
            jnp.dot(high, order, preferred_element_type=jnp.float32)
            + jnp.dot(mid, order, preferred_element_type=jnp.float32)
            + jnp.dot(low, order, preferred_element_type=jnp.float32)
        )
        for j in (0, 1):
            column = slice(j * half, (j + 1) * half)
            side[...] = y[:, column]
            for parity in (0, 1):
                out_ref[frame, parity * half : (parity + 1) * half, column] = side[
                    pl.ds(parity, half, stride=2), :
                ]
        return carry

    lax.fori_loop(0, facts[0, COUNT], permute, 0)


def frames_kernel(
    facts, field_ref, rim_ref, probe_ref, amp_ref, tables_ref,
    mine_ref, other_ref, own_ref, over_ref,
    ext, probe, amp, tables, win, xh, xl, fa, fb, total, grad, sems, out_sems,
):
    band = field_ref.shape[1]
    size = probe_ref.shape[1]
    half = size // 2
    steps = half // BLOCK
    count = facts[0, COUNT]

    pieces = []
    for c in (0, 1):
        for j in (0, 1):
            rows = slice(j * half, (j + 1) * half)
            pieces.append((field_ref.at[c, rows], ext.at[c, rows]))
            pieces.append((rim_ref.at[c, rows], ext.at[c, band + j * half : band + (j + 1) * half]))
    urgent = len(pieces)
    for c in (0, 1):
        pieces.append((probe_ref.at[c], probe.at[c]))
    for k in range(4):
        pieces.append((tables_ref.at[k], tables.at[k]))
        pieces.append((amp_ref.at[k], amp.at[k]))
    loads = [pltpu.make_async_copy(src, dst, sems.at[k]) for k, (src, dst) in enumerate(pieces)]
    for load in loads:
        load.start()
    total[...] = jnp.zeros_like(total)
    grad[...] = jnp.zeros_like(grad)
    for load in loads[: urgent + 2]:
        load.wait()

    def keep(b, which, place, value):
        high, low = split2(value)
        xh[(b, which, *place)] = high
        xl[(b, which, *place)] = low

    def by_right(b, which, table):
        high = xh[b, which]
        x = jnp.concatenate([high, xl[b, which], high], axis=1)
        t = tables[table, 0]
        t = jnp.concatenate([t, t, tables[table, 1]], axis=0)
        return jnp.dot(x, t, preferred_element_type=jnp.float32)

    def by_left(b, which, table):
        high = xh[b, which]
        x = jnp.concatenate([high, xl[b, which], high], axis=0)
        t = tables[table, 0]
        t = jnp.concatenate([t, t, tables[table, 1]], axis=1)
        return jnp.dot(t, x, preferred_element_type=jnp.float32)

    def cut(b, place):
        start, rest_row, base, rest_col = place

        def into(c):
            def use(i, rows_cut):
                win[b, c, i * BLOCK : (i + 1) * BLOCK, :] = rows_cut

            return use

        for c in (0, 1):
            read_window(
                lambda at, rows: ext[c, pl.ds(start + at, rows), pl.ds(base, 384)],
                size, rest_row, rest_col, into(c),
            )
        for i in range(size // BLOCK):
            row = slice(i * BLOCK, (i + 1) * BLOCK)
            wr, wi = win[b, 0, row, :], win[b, 1, row, :]
            pr, pi = probe[0, row, :], probe[1, row, :]
            er = pr * wr - pi * wi
            ei = pr * wi + pi * wr
            keep(b, 0, (row, slice(0, half)), er[:, :half] + er[:, half:])
            keep(b, 0, (row, slice(half, size)), ei[:, :half] + ei[:, half:])
            keep(b, 1, (row, slice(0, half)), er[:, :half] - er[:, half:])
            keep(b, 1, (row, slice(half, size)), ei[:, :half] - ei[:, half:])

    def right_forward(b):
        fa[b] = by_right(b, 0, 1)
        fb[b] = by_right(b, 1, 3)

    def fold_rows(b):
        for i in range(steps):
            top = slice(i * BLOCK, (i + 1) * BLOCK)
            low = slice(half + i * BLOCK, half + (i + 1) * BLOCK)
            for ref, out in ((fa, slice(0, half)), (fb, slice(half, size))):
                t, u = ref[b, top, :], ref[b, low, :]
                s, d = t + u, t - u
                keep(b, 0, (top, out), s[:, :half])
                keep(b, 0, (low, out), s[:, half:])
                keep(b, 1, (top, out), d[:, :half])
                keep(b, 1, (low, out), d[:, half:])

    def left_forward(b):
        fa[b] = by_left(b, 0, 0)
        fb[b] = by_left(b, 1, 2)

    def correct(b, frame, live):
        for i in range(steps):
            top = slice(i * BLOCK, (i + 1) * BLOCK)
            low = slice(half + i * BLOCK, half + (i + 1) * BLOCK)
            for which, ref in ((0, fa), (1, fb)):
                re, im = ref[b, top, :], ref[b, low, :]
                a = amp[frame, pl.ds(which * half + i * BLOCK, BLOCK), :]
                factor = 1.0 - a * lax.rsqrt(re * re + im * im + 0.25)
                factor = jnp.where(live, factor, 0.0)
                keep(b, which, (top, slice(0, size)), re * factor)
                keep(b, which, (low, slice(0, size)), im * factor)

    def left_back(b):
        fa[b] = by_left(b, 0, 1)
        fb[b] = by_left(b, 1, 3)

    def unfold_rows(b):
        for i in range(steps):
            top = slice(i * BLOCK, (i + 1) * BLOCK)
            low = slice(half + i * BLOCK, half + (i + 1) * BLOCK)
            for part, out in ((top, slice(0, half)), (low, slice(half, size))):
                p, q = fa[b, part, :], fb[b, part, :]
                s, d = p + q, p - q
                for place, v in ((top, s), (low, d)):
                    keep(b, 0, (place, out), v[:, :half])
                    keep(b, 1, (place, out), v[:, half:])

    def right_back(b):
        fa[b] = by_right(b, 0, 0)
        fb[b] = by_right(b, 1, 2)

    def spread(b, place):
        start, rest_row, base, rest_col = place
        before = [jnp.zeros((1, 8, 384), jnp.float32)] * 2
        for i in range(size // BLOCK):
            row = slice(i * BLOCK, (i + 1) * BLOCK)
            p, q = fa[b, row, :], fb[b, row, :]
            s, d = p + q, p - q
            br = jnp.concatenate([s[:, :half], d[:, :half]], axis=1)
            bi = jnp.concatenate([s[:, half:], d[:, half:]], axis=1)
            wr, wi = win[b, 0, row, :], win[b, 1, row, :]
            grad[0, row, :] = grad[0, row, :] + (wr * br + wi * bi)
            grad[1, row, :] = grad[1, row, :] + (wr * bi - wi * br)
            pr, pi = probe[0, row, :], probe[1, row, :]
            for c, v in ((0, pr * br + pi * bi), (1, pr * bi - pi * br)):
                part, before[c] = moved_rows(moved_columns(v, rest_col), before[c], rest_row)
                at = (c, pl.ds(start + i * BLOCK, BLOCK), pl.ds(base, 384))
                total[at] = total[at] + part
        for c in (0, 1):
            at = (c, pl.ds(start + size, 8), pl.ds(base, 384))
            total[at] = total[at] + last_rows(before[c], rest_row)

    def two_frames(pair, carry):
        frames = (2 * pair, 2 * pair + 1)
        places = [placed(*corner(facts, 0, frame)) for frame in frames]
        both = (0, 1)
        cut(0, places[0])

        @pl.when(pair == 0)
        def _():
            for load in loads[urgent + 2 :]:
                load.wait()

        right_forward(0)
        cut(1, places[1])
        right_forward(1)
        for elementwise, product in (
            (lambda b: fold_rows(b), left_forward),
            (lambda b: correct(b, frames[b], frames[b] < count), left_back),
            (lambda b: unfold_rows(b), right_back),
        ):
            for b in both:
                elementwise(b)
                product(b)
        for b in both:
            spread(b, places[b])
        return carry

    lax.fori_loop(0, (count + 1) // 2, two_frames, 0)
    stores = []
    for c in (0, 1):
        for j in (0, 1):
            rows = slice(j * half, (j + 1) * half)
            stores.append((total.at[c, band + j * half : band + (j + 1) * half], over_ref.at[c, rows]))
            stores.append((total.at[c, rows], own_ref.at[c, rows]))
    stores = [pltpu.make_async_copy(src, dst, out_sems.at[k]) for k, (src, dst) in enumerate(stores)]
    for store in stores:
        store.start()
    first = facts[0, CORE] == 0
    for i in range(size // BLOCK):
        row = slice(i * BLOCK, (i + 1) * BLOCK)
        re, im = grad[0, row, :], grad[1, row, :]
        mine_ref[row, :] = jnp.where(first, re, im)
        other_ref[row, :] = jnp.where(first, im, re)
    for store in stores:
        store.wait()


def update_kernel(facts, mine_ref, other_ref, probe_ref, out_ref):
    size = mine_ref.shape[0]
    mine, other = mine_ref[...], other_ref[...]
    squares = jnp.sum(mine * mine + other * other)
    step = 0.25 * lax.rsqrt(jnp.full((1, 1), squares / (2 * size * size) + 1e-06, jnp.float32))
    first = facts[0, CORE] == 0
    out_ref[0] = probe_ref[0] - step * jnp.where(first, mine, other)
    out_ref[1] = probe_ref[1] - step * jnp.where(first, other, mine)


def place_of(device):
    region, dev = divmod(device, 64)
    return {
        "x": region // 2,
        "z": (region % 2) * 4 + (dev // 2) % 4,
        "y": dev // 8,
        "core": dev % 2,
    }


def groups_along(by_core):
    groups = {}
    for device in range(512):
        place = place_of(device)
        key = tuple(v for k, v in place.items() if k not in by_core[place["core"]])
        groups.setdefault((place["core"], key), []).append(device)
    return list(groups.values())


def exchanged(parts, names):
    return lax.all_to_all(parts, AXES, 0, 0, tiled=True, axis_index_groups=groups_along(names))


def copies(part, names):
    peers = len(groups_along(names)[0])
    return exchanged(jnp.broadcast_to(part[None], (peers, *part.shape)), names)


def on_device(object_field, probe, amplitudes, row_offset, col_offset, frame_count):
    band, width = object_field.shape[1:]
    size = probe.shape[1]
    slots = amplitudes.shape[2]
    smem = pl.BlockSpec(memory_space=pltpu.SMEM)
    vmem = pl.BlockSpec(memory_space=pltpu.VMEM)
    hbm = pl.BlockSpec(memory_space=pltpu.HBM)
    f32 = jnp.float32
    peers = lax.axis_size("dev")

    rim = lax.ppermute(object_field, "dev", [(i, i - 1) for i in range(1, peers)])
    core = (lax.axis_index("dev") % 2).astype(jnp.int32)
    facts = jnp.concatenate([row_offset[0, 0], col_offset[0, 0], frame_count[0], core[None]])
    facts_before = lax.ppermute(facts, "dev", [(i, i + 1) for i in range(peers - 1)])
    facts = jnp.stack([facts, facts_before])

    ordered, scale = pl.pallas_call(
        prepare_kernel,
        out_shape=(
            jax.ShapeDtypeStruct((slots, size, size), f32),
            jax.ShapeDtypeStruct((band, width), f32),
        ),
        in_specs=[smem, vmem, vmem, vmem],
        out_specs=(vmem, vmem),
        scratch_shapes=[
            pltpu.VMEM((2 * band + size, width), f32),
            pltpu.VMEM((size, size // 2), f32),
        ],
        compiler_params=pltpu.CompilerParams(vmem_limit_bytes=65000 * 1024),
        cost_estimate=pl.CostEstimate(flops=800_000_000, bytes_accessed=3_200_000, transcendentals=0),
        name="prepare",
    )(facts, amplitudes[0, 0], probe, jnp.asarray(order_table(size)))

    bf16 = jnp.bfloat16
    mine, other, own, over = pl.pallas_call(
        frames_kernel,
        out_shape=(
            jax.ShapeDtypeStruct((size, size), f32),
            jax.ShapeDtypeStruct((size, size), f32),
            jax.ShapeDtypeStruct((2, band, width), f32),
            jax.ShapeDtypeStruct((2, size, width), f32),
        ),
        in_specs=[smem, hbm, hbm, hbm, hbm, hbm],
        out_specs=(vmem, vmem, hbm, hbm),
        scratch_shapes=[
            pltpu.VMEM((2, band + size, width), f32),
            pltpu.VMEM((2, size, size), f32),
            pltpu.VMEM((slots, size, size), f32),
            pltpu.VMEM((4, 2, size, size), bf16),
            pltpu.VMEM((2, 2, size, size), f32),
            pltpu.VMEM((2, 2, size, size), bf16),
            pltpu.VMEM((2, 2, size, size), bf16),
            pltpu.VMEM((2, size, size), f32),
            pltpu.VMEM((2, size, size), f32),
            pltpu.VMEM((2, band + size, width), f32),
            pltpu.VMEM((2, size, size), f32),
            pltpu.SemaphoreType.DMA((18,)),
            pltpu.SemaphoreType.DMA((8,)),
        ],
        compiler_params=pltpu.CompilerParams(vmem_limit_bytes=64500 * 1024),
        cost_estimate=pl.CostEstimate(flops=3_300_000_000, bytes_accessed=8_000_000, transcendentals=262144),
        name="frames",
    )(facts, object_field, rim, probe, ordered, jnp.asarray(frame_tables(size)))

    swap = [(i, i ^ 1) for i in range(peers)]
    plane = mine + lax.ppermute(other, "dev", swap)
    parts = exchanged(plane.reshape(32, size // 32, size), WIDE)
    share = jnp.sum(parts, axis=0)
    share = jnp.sum(copies(share, LINE), axis=0)
    plane = copies(share, WIDE).reshape(size, size)
    plane_other = lax.ppermute(plane, "dev", swap)

    incoming = lax.ppermute(over, "dev", [(i, i + 1) for i in range(peers - 1)])
    new_field = object_field - jnp.concatenate(
        [own[:, :size] + incoming, own[:, size:]], axis=1
    ) * scale[None]

    new_probe = pl.pallas_call(
        update_kernel,
        out_shape=jax.ShapeDtypeStruct(probe.shape, f32),
        in_specs=[smem, vmem, vmem, vmem],
        out_specs=vmem,
        compiler_params=pltpu.CompilerParams(vmem_limit_bytes=8 * 1024 * 1024),
        cost_estimate=pl.CostEstimate(flops=1_000_000, bytes_accessed=1_600_000, transcendentals=1),
        name="update",
    )(facts, plane, plane_other, probe)
    return (new_field, new_probe)


def solution(mesh):
    return jax.shard_map(
        on_device,
        mesh=mesh,
        in_specs=(
            P(None, ("region", "dev"), None),
            P(),
            P("region", "dev", None, None, None),
            P("region", "dev", None),
            P("region", "dev", None),
            P("region", "dev"),
        ),
        out_specs=(P(None, ("region", "dev"), None), P()),
        check_vma=False,
    )
```

```python
import numpy as np
import ml_dtypes

import jax
import jax.numpy as jnp
from jax import lax
from jax.experimental import pallas as pl
from jax.experimental.pallas import tpu as pltpu
from jax.sharding import PartitionSpec as P

AXES = ("region", "dev")
SLOTS = 4
COUNT, CORE = 2 * SLOTS, 2 * SLOTS + 1
BLOCK = 32
WIDE = (("x", "z"), ("x", "y"))
LINE = (("y",), ("z",))


def in_two(table):
    high = table.astype(ml_dtypes.bfloat16)
    low = (table - high.astype(np.float64)).astype(ml_dtypes.bfloat16)
    return high, low


def half_tables(length):
    half = length // 2
    k = np.arange(half)[:, None]
    n = np.arange(half)[None, :]
    forms = []
    for shift in (0, 1):
        turn = (n * (2 * k + shift)) % length
        angle = -2.0 * np.pi * turn / length
        real = np.cos(angle) / np.sqrt(length)
        imag = np.sin(angle) / np.sqrt(length)
        forms.append(np.block([[real, -imag], [imag, real]]))
    return forms


def frame_tables(length):
    first, second = half_tables(length)
    parts = [in_two(form) for form in (first, first.T, second, second.T)]
    return np.stack([np.stack(pair) for pair in parts])


def order_table(length):
    half = length // 2
    table = np.zeros((length, length), np.float32)
    table[2 * np.arange(half), np.arange(half)] = 1.0
    table[2 * np.arange(half) + 1, half + np.arange(half)] = 1.0
    return table.astype(ml_dtypes.bfloat16)


def split2(x):
    high = x.astype(jnp.bfloat16)
    low = (x - high.astype(jnp.float32)).astype(jnp.bfloat16)
    return high, low


def placed(row, col):
    block = jnp.minimum(col // 128, 1)
    return (
        pl.multiple_of(row // 8 * 8, 8),
        row % 8,
        pl.multiple_of(block * 128, 128),
        col - block * 128,
    )


def corner(facts, source, frame):
    return facts[source, frame], facts[source, SLOTS + frame]


def tiles(x):
    return x.reshape(x.shape[0] // 8, 8, x.shape[1])


def cut_columns(x, rest):
    shift = (128 - rest) & 127
    r = [pltpu.roll(x[:, 128 * j : 128 * j + 128], shift, axis=1) for j in range(3)]
    inside = lax.broadcasted_iota(jnp.int32, r[0].shape, 1) < 128 - rest
    return jnp.concatenate([jnp.where(inside, r[0], r[1]), jnp.where(inside, r[1], r[2])], axis=1)


def turned(x, shift):
    return pltpu.roll(tiles(x), shift & 7, axis=1)


def read_window(read, size, rest_row, rest_col, use):
    after = turned(cut_columns(read(size, 8), rest_col), 8 - rest_row)
    for i in reversed(range(size // BLOCK)):
        here = turned(cut_columns(read(i * BLOCK, BLOCK), rest_col), 8 - rest_row)
        later = jnp.concatenate([here[1:], after], axis=0)
        sub = lax.broadcasted_iota(jnp.int32, here.shape, 1)
        use(i, jnp.where(sub < 8 - rest_row, here, later).reshape(BLOCK, -1))
        after = here[:1]


def moved_columns(x, rest):
    shift = rest & 127
    ra = pltpu.roll(x[:, :128], shift, axis=1)
    rb = pltpu.roll(x[:, 128:], shift, axis=1)
    inside = lax.broadcasted_iota(jnp.int32, ra.shape, 1) >= rest
    zero = jnp.zeros_like(ra)
    return jnp.concatenate(
        [jnp.where(inside, ra, zero), jnp.where(inside, rb, ra), jnp.where(inside, zero, rb)], axis=1
    )


def moved_rows(x, before, rest_row):
    here = turned(x, rest_row)
    earlier = jnp.concatenate([before, here[:-1]], axis=0)
    sub = lax.broadcasted_iota(jnp.int32, here.shape, 1)
    return jnp.where(sub >= rest_row, here, earlier).reshape(x.shape), here[-1:]


def last_rows(before, rest_row):
    sub = lax.broadcasted_iota(jnp.int32, before.shape, 1)
    return jnp.where(sub >= rest_row, 0.0, before).reshape(8, -1)


def prepare_kernel(facts, amp_ref, probe_ref, order_ref, out_ref, weight_ref, total, side):
    band = weight_ref.shape[0]
    size = probe_ref.shape[1]
    half = size // 2
    total[...] = jnp.zeros_like(total)

    def add_power(source, frame, down):
        start, rest_row, base, rest_col = placed(*corner(facts, source, frame))
        before = jnp.zeros((1, 8, 384), jnp.float32)
        for i in range(size // BLOCK):
            pr = probe_ref[0, i * BLOCK : (i + 1) * BLOCK, :]
            pi = probe_ref[1, i * BLOCK : (i + 1) * BLOCK, :]
            part, before = moved_rows(moved_columns(pr * pr + pi * pi, rest_col), before, rest_row)
            place = (pl.ds(start + (down + i * BLOCK), BLOCK), pl.ds(base, 384))
            total[place] = total[place] + part
        place = (pl.ds(start + (down + size), 8), pl.ds(base, 384))
        total[place] = total[place] + last_rows(before, rest_row)

    def own(frame, carry):
        add_power(0, frame, band)
        return carry

    def previous(frame, carry):
        add_power(1, frame, 0)
        return carry

    lax.fori_loop(0, facts[0, COUNT], own, 0)
    lax.fori_loop(0, facts[1, COUNT], previous, 0)
    for i in range(band // BLOCK):
        weight_ref[i * BLOCK : (i + 1) * BLOCK, :] = 1.0 / (
            total[band + i * BLOCK : band + (i + 1) * BLOCK, :] + 1.0
        )

    def permute(frame, carry):
        x = amp_ref[frame]
        high = x.astype(jnp.bfloat16)
        left = x - high.astype(jnp.float32)
        mid = left.astype(jnp.bfloat16)
        low = (left - mid.astype(jnp.float32)).astype(jnp.bfloat16)
        order = order_ref[...]
        y = (
            jnp.dot(high, order, preferred_element_type=jnp.float32)
            + jnp.dot(mid, order, preferred_element_type=jnp.float32)
            + jnp.dot(low, order, preferred_element_type=jnp.float32)
        )
        for j in (0, 1):
            column = slice(j * half, (j + 1) * half)
            side[...] = y[:, column]
            for parity in (0, 1):
                out_ref[frame, parity * half : (parity + 1) * half, column] = side[
                    pl.ds(parity, half, stride=2), :
                ]
        return carry

    lax.fori_loop(0, facts[0, COUNT], permute, 0)


def frames_kernel(
    facts, field_ref, rim_ref, probe, amp, tables,
    mine_ref, other_ref, total,
    ext, win, xh, xl, fa, fb, grad, sems,
):
    band = field_ref.shape[1]
    size = probe.shape[1]
    half = size // 2
    steps = half // BLOCK
    count = facts[0, COUNT]

    loads = []
    for c in (0, 1):
        for j in (0, 1):
            rows = slice(j * half, (j + 1) * half)
            under = slice(band + j * half, band + (j + 1) * half)
            loads.append(
                pltpu.make_async_copy(rim_ref.at[c, rows], ext.at[c, under], sems.at[2 * c + j])
            )
    for load in loads:
        load.start()
    ext[:, :band] = field_ref[...]
    total[...] = jnp.zeros_like(total)
    grad[...] = jnp.zeros_like(grad)
    for load in loads:
        load.wait()

    def keep(b, which, place, value):
        high, low = split2(value)
        xh[(b, which, *place)] = high
        xl[(b, which, *place)] = low

    def by_right(b, which, table):
        high = xh[b, which]
        x = jnp.concatenate([high, xl[b, which], high], axis=1)
        t = tables[table, 0]
        t = jnp.concatenate([t, t, tables[table, 1]], axis=0)
        return jnp.dot(x, t, preferred_element_type=jnp.float32)

    def by_left(b, which, table):
        high = xh[b, which]
        x = jnp.concatenate([high, xl[b, which], high], axis=0)
        t = tables[table, 0]
        t = jnp.concatenate([t, t, tables[table, 1]], axis=1)
        return jnp.dot(t, x, preferred_element_type=jnp.float32)

    def cut(b, place):
        start, rest_row, base, rest_col = place

        def into(c):
            def use(i, rows_cut):
                win[b, c, i * BLOCK : (i + 1) * BLOCK, :] = rows_cut

            return use

        for c in (0, 1):
            read_window(
                lambda at, rows: ext[c, pl.ds(start + at, rows), pl.ds(base, 384)],
                size, rest_row, rest_col, into(c),
            )
        for i in range(size // BLOCK):
            row = slice(i * BLOCK, (i + 1) * BLOCK)
            wr, wi = win[b, 0, row, :], win[b, 1, row, :]
            pr, pi = probe[0, row, :], probe[1, row, :]
            er = pr * wr - pi * wi
            ei = pr * wi + pi * wr
            keep(b, 0, (row, slice(0, half)), er[:, :half] + er[:, half:])
            keep(b, 0, (row, slice(half, size)), ei[:, :half] + ei[:, half:])
            keep(b, 1, (row, slice(0, half)), er[:, :half] - er[:, half:])
            keep(b, 1, (row, slice(half, size)), ei[:, :half] - ei[:, half:])

    def right_forward(b):
        fa[b] = by_right(b, 0, 1)
        fb[b] = by_right(b, 1, 3)

    def fold_rows(b):
        for i in range(steps):
            top = slice(i * BLOCK, (i + 1) * BLOCK)
            low = slice(half + i * BLOCK, half + (i + 1) * BLOCK)
            for ref, out in ((fa, slice(0, half)), (fb, slice(half, size))):
                t, u = ref[b, top, :], ref[b, low, :]
                s, d = t + u, t - u
                keep(b, 0, (top, out), s[:, :half])
                keep(b, 0, (low, out), s[:, half:])
                keep(b, 1, (top, out), d[:, :half])
                keep(b, 1, (low, out), d[:, half:])

    def left_forward(b):
        fa[b] = by_left(b, 0, 0)
        fb[b] = by_left(b, 1, 2)

    def correct(b, frame, live):
        for i in range(steps):
            top = slice(i * BLOCK, (i + 1) * BLOCK)
            low = slice(half + i * BLOCK, half + (i + 1) * BLOCK)
            for which, ref in ((0, fa), (1, fb)):
                re, im = ref[b, top, :], ref[b, low, :]
                a = amp[frame, pl.ds(which * half + i * BLOCK, BLOCK), :]
                factor = 1.0 - a * lax.rsqrt(re * re + im * im + 0.25)
                factor = jnp.where(live, factor, 0.0)
                keep(b, which, (top, slice(0, size)), re * factor)
                keep(b, which, (low, slice(0, size)), im * factor)

    def left_back(b):
        fa[b] = by_left(b, 0, 1)
        fb[b] = by_left(b, 1, 3)

    def unfold_rows(b):
        for i in range(steps):
            top = slice(i * BLOCK, (i + 1) * BLOCK)
            low = slice(half + i * BLOCK, half + (i + 1) * BLOCK)
            for part, out in ((top, slice(0, half)), (low, slice(half, size))):
                p, q = fa[b, part, :], fb[b, part, :]
                s, d = p + q, p - q
                for place, v in ((top, s), (low, d)):
                    keep(b, 0, (place, out), v[:, :half])
                    keep(b, 1, (place, out), v[:, half:])

    def right_back(b):
        fa[b] = by_right(b, 0, 0)
        fb[b] = by_right(b, 1, 2)

    def spread(b, place):
        start, rest_row, base, rest_col = place
        before = [jnp.zeros((1, 8, 384), jnp.float32)] * 2
        for i in range(size // BLOCK):
            row = slice(i * BLOCK, (i + 1) * BLOCK)
            p, q = fa[b, row, :], fb[b, row, :]
            s, d = p + q, p - q
            br = jnp.concatenate([s[:, :half], d[:, :half]], axis=1)
            bi = jnp.concatenate([s[:, half:], d[:, half:]], axis=1)
            wr, wi = win[b, 0, row, :], win[b, 1, row, :]
            grad[0, row, :] = grad[0, row, :] + (wr * br + wi * bi)
            grad[1, row, :] = grad[1, row, :] + (wr * bi - wi * br)
            pr, pi = probe[0, row, :], probe[1, row, :]
            for c, v in ((0, pr * br + pi * bi), (1, pr * bi - pi * br)):
                part, before[c] = moved_rows(moved_columns(v, rest_col), before[c], rest_row)
                at = (c, pl.ds(start + i * BLOCK, BLOCK), pl.ds(base, 384))
                total[at] = total[at] + part
        for c in (0, 1):
            at = (c, pl.ds(start + size, 8), pl.ds(base, 384))
            total[at] = total[at] + last_rows(before[c], rest_row)

    def two_frames(pair, carry):
        frames = (2 * pair, 2 * pair + 1)
        places = [placed(*corner(facts, 0, frame)) for frame in frames]
        both = (0, 1)
        cut(0, places[0])
        right_forward(0)
        cut(1, places[1])
        right_forward(1)
        for elementwise, product in (
            (lambda b: fold_rows(b), left_forward),
            (lambda b: correct(b, frames[b], frames[b] < count), left_back),
            (lambda b: unfold_rows(b), right_back),
        ):
            for b in both:
                elementwise(b)
                product(b)
        for b in both:
            spread(b, places[b])
        return carry

    lax.fori_loop(0, (count + 1) // 2, two_frames, 0)
    first = facts[0, CORE] == 0
    for i in range(size // BLOCK):
        row = slice(i * BLOCK, (i + 1) * BLOCK)
        re, im = grad[0, row, :], grad[1, row, :]
        mine_ref[row, :] = jnp.where(first, re, im)
        other_ref[row, :] = jnp.where(first, im, re)


def update_kernel(facts, mine_ref, other_ref, probe_ref, out_ref):
    size = mine_ref.shape[0]
    mine, other = mine_ref[...], other_ref[...]
    squares = jnp.sum(mine * mine + other * other)
    step = 0.25 * lax.rsqrt(jnp.full((1, 1), squares / (2 * size * size) + 1e-06, jnp.float32))
    first = facts[0, CORE] == 0
    out_ref[0] = probe_ref[0] - step * jnp.where(first, mine, other)
    out_ref[1] = probe_ref[1] - step * jnp.where(first, other, mine)


def place_of(device):
    region, dev = divmod(device, 64)
    return {
        "x": region // 2,
        "z": (region % 2) * 4 + (dev // 2) % 4,
        "y": dev // 8,
        "core": dev % 2,
    }


def groups_along(by_core):
    groups = {}
    for device in range(512):
        place = place_of(device)
        key = tuple(v for k, v in place.items() if k not in by_core[place["core"]])
        groups.setdefault((place["core"], key), []).append(device)
    return list(groups.values())


def exchanged(parts, names):
    return lax.all_to_all(parts, AXES, 0, 0, tiled=True, axis_index_groups=groups_along(names))


def copies(part, names):
    peers = len(groups_along(names)[0])
    return exchanged(jnp.broadcast_to(part[None], (peers, *part.shape)), names)


def on_device(object_field, probe, amplitudes, row_offset, col_offset, frame_count):
    band, width = object_field.shape[1:]
    size = probe.shape[1]
    slots = amplitudes.shape[2]
    smem = pl.BlockSpec(memory_space=pltpu.SMEM)
    vmem = pl.BlockSpec(memory_space=pltpu.VMEM)
    hbm = pl.BlockSpec(memory_space=pltpu.HBM)
    f32 = jnp.float32
    peers = lax.axis_size("dev")

    rim = lax.ppermute(object_field, "dev", [(i, i - 1) for i in range(1, peers)])
    rim = pltpu.with_memory_space_constraint(rim, pltpu.HBM)
    core = (lax.axis_index("dev") % 2).astype(jnp.int32)
    facts = jnp.concatenate([row_offset[0, 0], col_offset[0, 0], frame_count[0], core[None]])
    facts_before = lax.ppermute(facts, "dev", [(i, i + 1) for i in range(peers - 1)])
    facts = jnp.stack([facts, facts_before])

    ordered, scale = pl.pallas_call(
        prepare_kernel,
        out_shape=(
            jax.ShapeDtypeStruct((slots, size, size), f32),
            jax.ShapeDtypeStruct((band, width), f32),
        ),
        in_specs=[smem, vmem, vmem, vmem],
        out_specs=(vmem, vmem),
        scratch_shapes=[
            pltpu.VMEM((2 * band + size, width), f32),
            pltpu.VMEM((size, size // 2), f32),
        ],
        compiler_params=pltpu.CompilerParams(vmem_limit_bytes=24000 * 1024),
        cost_estimate=pl.CostEstimate(flops=800_000_000, bytes_accessed=3_200_000, transcendentals=0),
        name="prepare",
    )(facts, amplitudes[0, 0], probe, jnp.asarray(order_table(size)))

    bf16 = jnp.bfloat16
    mine, other, total = pl.pallas_call(
        frames_kernel,
        out_shape=(
            jax.ShapeDtypeStruct((size, size), f32),
            jax.ShapeDtypeStruct((size, size), f32),
            jax.ShapeDtypeStruct((2, band + size, width), f32),
        ),
        in_specs=[smem, vmem, hbm, vmem, vmem, vmem],
        out_specs=(vmem, vmem, vmem),
        scratch_shapes=[
            pltpu.VMEM((2, band + size, width), f32),
            pltpu.VMEM((2, 2, size, size), f32),
            pltpu.VMEM((2, 2, size, size), bf16),
            pltpu.VMEM((2, 2, size, size), bf16),
            pltpu.VMEM((2, size, size), f32),
            pltpu.VMEM((2, size, size), f32),
            pltpu.VMEM((2, size, size), f32),
            pltpu.SemaphoreType.DMA((4,)),
        ],
        compiler_params=pltpu.CompilerParams(vmem_limit_bytes=24 * 1024 * 1024),
        cost_estimate=pl.CostEstimate(flops=3_300_000_000, bytes_accessed=8_000_000, transcendentals=262144),
        name="frames",
    )(facts, object_field, rim, probe, ordered, jnp.asarray(frame_tables(size)))
    own, over = total[:, :band], total[:, band:]

    swap = [(i, i ^ 1) for i in range(peers)]
    plane = mine + lax.ppermute(other, "dev", swap)
    parts = exchanged(plane.reshape(32, size // 32, size), WIDE)
    share = jnp.sum(parts, axis=0)
    share = jnp.sum(copies(share, LINE), axis=0)
    plane = copies(share, WIDE).reshape(size, size)
    plane_other = lax.ppermute(plane, "dev", swap)

    incoming = lax.ppermute(over, "dev", [(i, i + 1) for i in range(peers - 1)])
    new_field = object_field - jnp.concatenate(
        [own[:, :size] + incoming, own[:, size:]], axis=1
    ) * scale[None]

    new_probe = pl.pallas_call(
        update_kernel,
        out_shape=jax.ShapeDtypeStruct(probe.shape, f32),
        in_specs=[smem, vmem, vmem, vmem],
        out_specs=vmem,
        compiler_params=pltpu.CompilerParams(vmem_limit_bytes=8 * 1024 * 1024),
        cost_estimate=pl.CostEstimate(flops=1_000_000, bytes_accessed=1_600_000, transcendentals=1),
        name="update",
    )(facts, plane, plane_other, probe)
    return (new_field, new_probe)


def solution(mesh):
    return jax.shard_map(
        on_device,
        mesh=mesh,
        in_specs=(
            P(None, ("region", "dev"), None),
            P(),
            P("region", "dev", None, None, None),
            P("region", "dev", None),
            P("region", "dev", None),
            P("region", "dev"),
        ),
        out_specs=(P(None, ("region", "dev"), None), P()),
        check_vma=False,
    )
```

```python
import numpy as np
import ml_dtypes

import jax
import jax.numpy as jnp
from jax import lax
from jax.experimental import pallas as pl
from jax.experimental.pallas import tpu as pltpu
from jax.sharding import PartitionSpec as P

AXES = ("region", "dev")
SLOTS = 4
COUNT, CORE = 2 * SLOTS, 2 * SLOTS + 1
BLOCK = 32
WIDE = (("x", "z"), ("x", "y"))
LINE = (("y",), ("z",))


def in_two(table):
    high = table.astype(ml_dtypes.bfloat16)
    low = (table - high.astype(np.float64)).astype(ml_dtypes.bfloat16)
    return high, low


def half_tables(length):
    half = length // 2
    k = np.arange(half)[:, None]
    n = np.arange(half)[None, :]
    forms = []
    for shift in (0, 1):
        turn = (n * (2 * k + shift)) % length
        angle = -2.0 * np.pi * turn / length
        real = np.cos(angle) / np.sqrt(length)
        imag = np.sin(angle) / np.sqrt(length)
        forms.append(np.block([[real, -imag], [imag, real]]))
    return forms


def frame_tables(length):
    first, second = half_tables(length)
    parts = [in_two(form) for form in (first, first.T, second, second.T)]
    return np.stack([np.stack(pair) for pair in parts])


def order_table(length):
    half = length // 2
    table = np.zeros((length, length), np.float32)
    table[2 * np.arange(half), np.arange(half)] = 1.0
    table[2 * np.arange(half) + 1, half + np.arange(half)] = 1.0
    return table.astype(ml_dtypes.bfloat16)


def split2(x):
    high = x.astype(jnp.bfloat16)
    low = (x - high.astype(jnp.float32)).astype(jnp.bfloat16)
    return high, low


def placed(row, col):
    block = jnp.minimum(col // 128, 1)
    return (
        pl.multiple_of(row // 8 * 8, 8),
        row % 8,
        pl.multiple_of(block * 128, 128),
        col - block * 128,
    )


def corner(facts, source, frame):
    return facts[source, frame], facts[source, SLOTS + frame]


def tiles(x):
    return x.reshape(x.shape[0] // 8, 8, x.shape[1])


def cut_columns(x, rest):
    shift = (128 - rest) & 127
    r = [pltpu.roll(x[:, 128 * j : 128 * j + 128], shift, axis=1) for j in range(3)]
    inside = lax.broadcasted_iota(jnp.int32, r[0].shape, 1) < 128 - rest
    return jnp.concatenate([jnp.where(inside, r[0], r[1]), jnp.where(inside, r[1], r[2])], axis=1)


def turned(x, shift):
    return pltpu.roll(tiles(x), shift & 7, axis=1)


def read_window(read, size, rest_row, rest_col, use):
    after = turned(cut_columns(read(size, 8), rest_col), 8 - rest_row)
    for i in reversed(range(size // BLOCK)):
        here = turned(cut_columns(read(i * BLOCK, BLOCK), rest_col), 8 - rest_row)
        later = jnp.concatenate([here[1:], after], axis=0)
        sub = lax.broadcasted_iota(jnp.int32, here.shape, 1)
        use(i, jnp.where(sub < 8 - rest_row, here, later).reshape(BLOCK, -1))
        after = here[:1]


def moved_columns(x, rest):
    shift = rest & 127
    ra = pltpu.roll(x[:, :128], shift, axis=1)
    rb = pltpu.roll(x[:, 128:], shift, axis=1)
    inside = lax.broadcasted_iota(jnp.int32, ra.shape, 1) >= rest
    zero = jnp.zeros_like(ra)
    return jnp.concatenate(
        [jnp.where(inside, ra, zero), jnp.where(inside, rb, ra), jnp.where(inside, zero, rb)], axis=1
    )


def moved_rows(x, before, rest_row):
    here = turned(x, rest_row)
    earlier = jnp.concatenate([before, here[:-1]], axis=0)
    sub = lax.broadcasted_iota(jnp.int32, here.shape, 1)
    return jnp.where(sub >= rest_row, here, earlier).reshape(x.shape), here[-1:]


def last_rows(before, rest_row):
    sub = lax.broadcasted_iota(jnp.int32, before.shape, 1)
    return jnp.where(sub >= rest_row, 0.0, before).reshape(8, -1)


def prepare_kernel(facts, amp_ref, probe_ref, order_ref, out_ref, weight_ref, total, side):
    band = weight_ref.shape[0]
    size = probe_ref.shape[1]
    half = size // 2
    total[...] = jnp.zeros_like(total)

    def add_power(source, frame, down):
        start, rest_row, base, rest_col = placed(*corner(facts, source, frame))
        before = jnp.zeros((1, 8, 384), jnp.float32)
        for i in range(size // BLOCK):
            pr = probe_ref[0, i * BLOCK : (i + 1) * BLOCK, :]
            pi = probe_ref[1, i * BLOCK : (i + 1) * BLOCK, :]
            part, before = moved_rows(moved_columns(pr * pr + pi * pi, rest_col), before, rest_row)
            place = (pl.ds(start + (down + i * BLOCK), BLOCK), pl.ds(base, 384))
            total[place] = total[place] + part
        place = (pl.ds(start + (down + size), 8), pl.ds(base, 384))
        total[place] = total[place] + last_rows(before, rest_row)

    def own(frame, carry):
        add_power(0, frame, band)
        return carry

    def previous(frame, carry):
        add_power(1, frame, 0)
        return carry

    lax.fori_loop(0, facts[0, COUNT], own, 0)
    lax.fori_loop(0, facts[1, COUNT], previous, 0)
    for i in range(band // BLOCK):
        weight_ref[i * BLOCK : (i + 1) * BLOCK, :] = 1.0 / (
            total[band + i * BLOCK : band + (i + 1) * BLOCK, :] + 1.0
        )

    def permute(frame, carry):
        x = amp_ref[frame]
        high = x.astype(jnp.bfloat16)
        left = x - high.astype(jnp.float32)
        mid = left.astype(jnp.bfloat16)
        low = (left - mid.astype(jnp.float32)).astype(jnp.bfloat16)
        order = order_ref[...]
        y = (
            jnp.dot(high, order, preferred_element_type=jnp.float32)
            + jnp.dot(mid, order, preferred_element_type=jnp.float32)
            + jnp.dot(low, order, preferred_element_type=jnp.float32)
        )
        for j in (0, 1):
            column = slice(j * half, (j + 1) * half)
            side[...] = y[:, column]
            for parity in (0, 1):
                out_ref[frame, parity * half : (parity + 1) * half, column] = side[
                    pl.ds(parity, half, stride=2), :
                ]
        return carry

    lax.fori_loop(0, facts[0, COUNT], permute, 0)


def frames_kernel(
    facts, ext, probe, amp, tables,
    mine_ref, other_ref, total,
    win, xh, xl, fa, fb, grad,
):
    size = probe.shape[1]
    half = size // 2
    steps = half // BLOCK
    count = facts[0, COUNT]

    total[...] = jnp.zeros_like(total)
    grad[...] = jnp.zeros_like(grad)

    def keep(b, which, place, value):
        high, low = split2(value)
        xh[(b, which, *place)] = high
        xl[(b, which, *place)] = low

    def by_right(b, which, table):
        high = xh[b, which]
        x = jnp.concatenate([high, xl[b, which], high], axis=1)
        t = tables[table, 0]
        t = jnp.concatenate([t, t, tables[table, 1]], axis=0)
        return jnp.dot(x, t, preferred_element_type=jnp.float32)

    def by_left(b, which, table):
        high = xh[b, which]
        x = jnp.concatenate([high, xl[b, which], high], axis=0)
        t = tables[table, 0]
        t = jnp.concatenate([t, t, tables[table, 1]], axis=1)
        return jnp.dot(t, x, preferred_element_type=jnp.float32)

    def cut(b, place):
        start, rest_row, base, rest_col = place

        def into(c):
            def use(i, rows_cut):
                win[b, c, i * BLOCK : (i + 1) * BLOCK, :] = rows_cut

            return use

        for c in (0, 1):
            read_window(
                lambda at, rows: ext[c, pl.ds(start + at, rows), pl.ds(base, 384)],
                size, rest_row, rest_col, into(c),
            )
        for i in range(size // BLOCK):
            row = slice(i * BLOCK, (i + 1) * BLOCK)
            wr, wi = win[b, 0, row, :], win[b, 1, row, :]
            pr, pi = probe[0, row, :], probe[1, row, :]
            er = pr * wr - pi * wi
            ei = pr * wi + pi * wr
            keep(b, 0, (row, slice(0, half)), er[:, :half] + er[:, half:])
            keep(b, 0, (row, slice(half, size)), ei[:, :half] + ei[:, half:])
            keep(b, 1, (row, slice(0, half)), er[:, :half] - er[:, half:])
            keep(b, 1, (row, slice(half, size)), ei[:, :half] - ei[:, half:])

    def right_forward(b):
        fa[b] = by_right(b, 0, 1)
        fb[b] = by_right(b, 1, 3)

    def fold_rows(b):
        for i in range(steps):
            top = slice(i * BLOCK, (i + 1) * BLOCK)
            low = slice(half + i * BLOCK, half + (i + 1) * BLOCK)
            for ref, out in ((fa, slice(0, half)), (fb, slice(half, size))):
                t, u = ref[b, top, :], ref[b, low, :]
                s, d = t + u, t - u
                keep(b, 0, (top, out), s[:, :half])
                keep(b, 0, (low, out), s[:, half:])
                keep(b, 1, (top, out), d[:, :half])
                keep(b, 1, (low, out), d[:, half:])

    def left_forward(b):
        fa[b] = by_left(b, 0, 0)
        fb[b] = by_left(b, 1, 2)

    def correct(b, frame, live):
        for i in range(steps):
            top = slice(i * BLOCK, (i + 1) * BLOCK)
            low = slice(half + i * BLOCK, half + (i + 1) * BLOCK)
            for which, ref in ((0, fa), (1, fb)):
                re, im = ref[b, top, :], ref[b, low, :]
                a = amp[frame, pl.ds(which * half + i * BLOCK, BLOCK), :]
                factor = 1.0 - a * lax.rsqrt(re * re + im * im + 0.25)
                factor = jnp.where(live, factor, 0.0)
                keep(b, which, (top, slice(0, size)), re * factor)
                keep(b, which, (low, slice(0, size)), im * factor)

    def left_back(b):
        fa[b] = by_left(b, 0, 1)
        fb[b] = by_left(b, 1, 3)

    def unfold_rows(b):
        for i in range(steps):
            top = slice(i * BLOCK, (i + 1) * BLOCK)
            low = slice(half + i * BLOCK, half + (i + 1) * BLOCK)
            for part, out in ((top, slice(0, half)), (low, slice(half, size))):
                p, q = fa[b, part, :], fb[b, part, :]
                s, d = p + q, p - q
                for place, v in ((top, s), (low, d)):
                    keep(b, 0, (place, out), v[:, :half])
                    keep(b, 1, (place, out), v[:, half:])

    def right_back(b):
        fa[b] = by_right(b, 0, 0)
        fb[b] = by_right(b, 1, 2)

    def spread(b, place):
        start, rest_row, base, rest_col = place
        before = [jnp.zeros((1, 8, 384), jnp.float32)] * 2
        for i in range(size // BLOCK):
            row = slice(i * BLOCK, (i + 1) * BLOCK)
            p, q = fa[b, row, :], fb[b, row, :]
            s, d = p + q, p - q
            br = jnp.concatenate([s[:, :half], d[:, :half]], axis=1)
            bi = jnp.concatenate([s[:, half:], d[:, half:]], axis=1)
            wr, wi = win[b, 0, row, :], win[b, 1, row, :]
            grad[0, row, :] = grad[0, row, :] + (wr * br + wi * bi)
            grad[1, row, :] = grad[1, row, :] + (wr * bi - wi * br)
            pr, pi = probe[0, row, :], probe[1, row, :]
            for c, v in ((0, pr * br + pi * bi), (1, pr * bi - pi * br)):
                part, before[c] = moved_rows(moved_columns(v, rest_col), before[c], rest_row)
                at = (c, pl.ds(start + i * BLOCK, BLOCK), pl.ds(base, 384))
                total[at] = total[at] + part
        for c in (0, 1):
            at = (c, pl.ds(start + size, 8), pl.ds(base, 384))
            total[at] = total[at] + last_rows(before[c], rest_row)

    def two_frames(pair, carry):
        frames = (2 * pair, 2 * pair + 1)
        places = [placed(*corner(facts, 0, frame)) for frame in frames]
        both = (0, 1)
        cut(0, places[0])
        right_forward(0)
        cut(1, places[1])
        right_forward(1)
        for elementwise, product in (
            (lambda b: fold_rows(b), left_forward),
            (lambda b: correct(b, frames[b], frames[b] < count), left_back),
            (lambda b: unfold_rows(b), right_back),
        ):
            for b in both:
                elementwise(b)
                product(b)
        for b in both:
            spread(b, places[b])
        return carry

    lax.fori_loop(0, (count + 1) // 2, two_frames, 0)
    first = facts[0, CORE] == 0
    for i in range(size // BLOCK):
        row = slice(i * BLOCK, (i + 1) * BLOCK)
        re, im = grad[0, row, :], grad[1, row, :]
        mine_ref[row, :] = jnp.where(first, re, im)
        other_ref[row, :] = jnp.where(first, im, re)


def update_kernel(facts, mine_ref, other_ref, probe_ref, out_ref):
    size = mine_ref.shape[0]
    mine, other = mine_ref[...], other_ref[...]
    squares = jnp.sum(mine * mine + other * other)
    step = 0.25 * lax.rsqrt(jnp.full((1, 1), squares / (2 * size * size) + 1e-06, jnp.float32))
    first = facts[0, CORE] == 0
    out_ref[0] = probe_ref[0] - step * jnp.where(first, mine, other)
    out_ref[1] = probe_ref[1] - step * jnp.where(first, other, mine)


def place_of(device):
    region, dev = divmod(device, 64)
    return {
        "x": region // 2,
        "z": (region % 2) * 4 + (dev // 2) % 4,
        "y": dev // 8,
        "core": dev % 2,
    }


def groups_along(by_core):
    groups = {}
    for device in range(512):
        place = place_of(device)
        key = tuple(v for k, v in place.items() if k not in by_core[place["core"]])
        groups.setdefault((place["core"], key), []).append(device)
    return list(groups.values())


def exchanged(parts, names):
    return lax.all_to_all(parts, AXES, 0, 0, tiled=True, axis_index_groups=groups_along(names))


def copies(part, names):
    peers = len(groups_along(names)[0])
    return exchanged(jnp.broadcast_to(part[None], (peers, *part.shape)), names)


def on_device(object_field, probe, amplitudes, row_offset, col_offset, frame_count):
    band, width = object_field.shape[1:]
    size = probe.shape[1]
    slots = amplitudes.shape[2]
    smem = pl.BlockSpec(memory_space=pltpu.SMEM)
    vmem = pl.BlockSpec(memory_space=pltpu.VMEM)
    hbm = pl.BlockSpec(memory_space=pltpu.HBM)
    f32 = jnp.float32
    peers = lax.axis_size("dev")

    rim = lax.ppermute(object_field, "dev", [(i, i - 1) for i in range(1, peers)])
    core = (lax.axis_index("dev") % 2).astype(jnp.int32)
    facts = jnp.concatenate([row_offset[0, 0], col_offset[0, 0], frame_count[0], core[None]])
    facts_before = lax.ppermute(facts, "dev", [(i, i + 1) for i in range(peers - 1)])
    facts = jnp.stack([facts, facts_before])

    ordered, scale = pl.pallas_call(
        prepare_kernel,
        out_shape=(
            jax.ShapeDtypeStruct((slots, size, size), f32),
            jax.ShapeDtypeStruct((band, width), f32),
        ),
        in_specs=[smem, vmem, vmem, vmem],
        out_specs=(vmem, vmem),
        scratch_shapes=[
            pltpu.VMEM((2 * band + size, width), f32),
            pltpu.VMEM((size, size // 2), f32),
        ],
        compiler_params=pltpu.CompilerParams(vmem_limit_bytes=24000 * 1024),
        cost_estimate=pl.CostEstimate(flops=800_000_000, bytes_accessed=3_200_000, transcendentals=0),
        name="prepare",
    )(facts, amplitudes[0, 0], probe, jnp.asarray(order_table(size)))

    bf16 = jnp.bfloat16
    ext = jnp.pad(object_field, ((0, 0), (0, size), (0, 0)))
    ext, rim = lax.optimization_barrier((ext, rim))
    ext = lax.dynamic_update_slice(ext, rim[:, :size], (0, band, 0))
    mine, other, total = pl.pallas_call(
        frames_kernel,
        out_shape=(
            jax.ShapeDtypeStruct((size, size), f32),
            jax.ShapeDtypeStruct((size, size), f32),
            jax.ShapeDtypeStruct((2, band + size, width), f32),
        ),
        in_specs=[smem, vmem, vmem, vmem, vmem],
        out_specs=(vmem, vmem, vmem),
        scratch_shapes=[
            pltpu.VMEM((2, 2, size, size), f32),
            pltpu.VMEM((2, 2, size, size), bf16),
            pltpu.VMEM((2, 2, size, size), bf16),
            pltpu.VMEM((2, size, size), f32),
            pltpu.VMEM((2, size, size), f32),
            pltpu.VMEM((2, size, size), f32),
        ],
        compiler_params=pltpu.CompilerParams(vmem_limit_bytes=24 * 1024 * 1024),
        cost_estimate=pl.CostEstimate(flops=3_300_000_000, bytes_accessed=8_000_000, transcendentals=262144),
        name="frames",
    )(facts, ext, probe, ordered, jnp.asarray(frame_tables(size)))
    over = total[:, band:]
    steps = [(i, i + 1) for i in range(peers - 1)]
    swap = [(i, i ^ 1) for i in range(peers)]
    plane = mine + lax.ppermute(other, "dev", swap)
    incoming = lax.ppermute(over, "dev", steps)
    parts = exchanged(plane.reshape(32, size // 32, size), WIDE)
    share = jnp.sum(parts, axis=0)
    share = jnp.sum(copies(share, LINE), axis=0)
    share, total = lax.optimization_barrier((share, total))
    own = total[:, :band]
    new_field = object_field - jnp.concatenate(
        [own[:, :size] + incoming, own[:, size:]], axis=1
    ) * scale[None]
    plane = copies(share, WIDE).reshape(size, size)
    plane, new_field = lax.optimization_barrier((plane, new_field))
    plane_other = lax.ppermute(plane, "dev", swap)

    new_probe = pl.pallas_call(
        update_kernel,
        out_shape=jax.ShapeDtypeStruct(probe.shape, f32),
        in_specs=[smem, vmem, vmem, vmem],
        out_specs=vmem,
        compiler_params=pltpu.CompilerParams(vmem_limit_bytes=8 * 1024 * 1024),
        cost_estimate=pl.CostEstimate(flops=1_000_000, bytes_accessed=1_600_000, transcendentals=1),
        name="update",
    )(facts, plane, plane_other, probe)
    return (new_field, new_probe)


def solution(mesh):
    return jax.shard_map(
        on_device,
        mesh=mesh,
        in_specs=(
            P(None, ("region", "dev"), None),
            P(),
            P("region", "dev", None, None, None),
            P("region", "dev", None),
            P("region", "dev", None),
            P("region", "dev"),
        ),
        out_specs=(P(None, ("region", "dev"), None), P()),
        check_vma=False,
    )
```

```python
import numpy as np
import ml_dtypes

import jax
import jax.numpy as jnp
from jax import lax
from jax.experimental import pallas as pl
from jax.experimental.pallas import tpu as pltpu
from jax.sharding import PartitionSpec as P

AXES = ("region", "dev")
SLOTS = 4
COUNT, CORE = 2 * SLOTS, 2 * SLOTS + 1
BLOCK = 32
WIDE = (("x", "z"), ("x", "y"))
LINE = (("y",), ("z",))


def in_two(table):
    high = table.astype(ml_dtypes.bfloat16)
    low = (table - high.astype(np.float64)).astype(ml_dtypes.bfloat16)
    return high, low


def half_tables(length):
    half = length // 2
    k = np.arange(half)[:, None]
    n = np.arange(half)[None, :]
    forms = []
    for shift in (0, 1):
        turn = (n * (2 * k + shift)) % length
        angle = -2.0 * np.pi * turn / length
        real = np.cos(angle) / np.sqrt(length)
        imag = np.sin(angle) / np.sqrt(length)
        forms.append(np.block([[real, -imag], [imag, real]]))
    return forms


def frame_tables(length):
    first, second = half_tables(length)
    parts = [in_two(form) for form in (first, first.T, second, second.T)]
    return np.stack([np.stack(pair) for pair in parts])


def order_table(length):
    half = length // 2
    table = np.zeros((length, length), np.float32)
    table[2 * np.arange(half), np.arange(half)] = 1.0
    table[2 * np.arange(half) + 1, half + np.arange(half)] = 1.0
    return table.astype(ml_dtypes.bfloat16)


def split2(x):
    high = x.astype(jnp.bfloat16)
    low = (x - high.astype(jnp.float32)).astype(jnp.bfloat16)
    return high, low


def placed(row, col):
    block = jnp.minimum(col // 128, 1)
    return (
        pl.multiple_of(row // 8 * 8, 8),
        row % 8,
        pl.multiple_of(block * 128, 128),
        col - block * 128,
    )


def corner(facts, source, frame):
    return facts[source, frame], facts[source, SLOTS + frame]


def tiles(x):
    return x.reshape(x.shape[0] // 8, 8, x.shape[1])


def cut_columns(x, rest):
    shift = (128 - rest) & 127
    r = [pltpu.roll(x[:, 128 * j : 128 * j + 128], shift, axis=1) for j in range(3)]
    inside = lax.broadcasted_iota(jnp.int32, r[0].shape, 1) < 128 - rest
    return jnp.concatenate([jnp.where(inside, r[0], r[1]), jnp.where(inside, r[1], r[2])], axis=1)


def turned(x, shift):
    return pltpu.roll(tiles(x), shift & 7, axis=1)


def read_window(read, size, rest_row, rest_col, use):
    after = turned(cut_columns(read(size, 8), rest_col), 8 - rest_row)
    for i in reversed(range(size // BLOCK)):
        here = turned(cut_columns(read(i * BLOCK, BLOCK), rest_col), 8 - rest_row)
        later = jnp.concatenate([here[1:], after], axis=0)
        sub = lax.broadcasted_iota(jnp.int32, here.shape, 1)
        use(i, jnp.where(sub < 8 - rest_row, here, later).reshape(BLOCK, -1))
        after = here[:1]


def moved_columns(x, rest):
    shift = rest & 127
    ra = pltpu.roll(x[:, :128], shift, axis=1)
    rb = pltpu.roll(x[:, 128:], shift, axis=1)
    inside = lax.broadcasted_iota(jnp.int32, ra.shape, 1) >= rest
    zero = jnp.zeros_like(ra)
    return jnp.concatenate(
        [jnp.where(inside, ra, zero), jnp.where(inside, rb, ra), jnp.where(inside, zero, rb)], axis=1
    )


def moved_rows(x, before, rest_row):
    here = turned(x, rest_row)
    earlier = jnp.concatenate([before, here[:-1]], axis=0)
    sub = lax.broadcasted_iota(jnp.int32, here.shape, 1)
    return jnp.where(sub >= rest_row, here, earlier).reshape(x.shape), here[-1:]


def last_rows(before, rest_row):
    sub = lax.broadcasted_iota(jnp.int32, before.shape, 1)
    return jnp.where(sub >= rest_row, 0.0, before).reshape(8, -1)


def prepare_kernel(facts, amp_ref, probe_ref, order_ref, out_ref, weight_ref, total, side):
    band = weight_ref.shape[0]
    size = probe_ref.shape[1]
    half = size // 2
    total[...] = jnp.zeros_like(total)

    def add_power(source, frame, down):
        start, rest_row, base, rest_col = placed(*corner(facts, source, frame))
        before = jnp.zeros((1, 8, 384), jnp.float32)
        for i in range(size // BLOCK):
            pr = probe_ref[0, i * BLOCK : (i + 1) * BLOCK, :]
            pi = probe_ref[1, i * BLOCK : (i + 1) * BLOCK, :]
            part, before = moved_rows(moved_columns(pr * pr + pi * pi, rest_col), before, rest_row)
            place = (pl.ds(start + (down + i * BLOCK), BLOCK), pl.ds(base, 384))
            total[place] = total[place] + part
        place = (pl.ds(start + (down + size), 8), pl.ds(base, 384))
        total[place] = total[place] + last_rows(before, rest_row)

    def own(frame, carry):
        add_power(0, frame, band)
        return carry

    def previous(frame, carry):
        add_power(1, frame, 0)
        return carry

    lax.fori_loop(0, facts[0, COUNT], own, 0)
    lax.fori_loop(0, facts[1, COUNT], previous, 0)
    for i in range(band // BLOCK):
        weight_ref[i * BLOCK : (i + 1) * BLOCK, :] = 1.0 / (
            total[band + i * BLOCK : band + (i + 1) * BLOCK, :] + 1.0
        )

    def permute(frame, carry):
        x = amp_ref[frame]
        high = x.astype(jnp.bfloat16)
        left = x - high.astype(jnp.float32)
        mid = left.astype(jnp.bfloat16)
        low = (left - mid.astype(jnp.float32)).astype(jnp.bfloat16)
        order = order_ref[...]
        y = (
            jnp.dot(high, order, preferred_element_type=jnp.float32)
            + jnp.dot(mid, order, preferred_element_type=jnp.float32)
            + jnp.dot(low, order, preferred_element_type=jnp.float32)
        )
        for j in (0, 1):
            column = slice(j * half, (j + 1) * half)
            side[...] = y[:, column]
            for parity in (0, 1):
                out_ref[frame, parity * half : (parity + 1) * half, column] = side[
                    pl.ds(parity, half, stride=2), :
                ]
        return carry

    lax.fori_loop(0, facts[0, COUNT], permute, 0)


def frames_kernel(
    facts, ext, probe, amp, tables,
    mine_ref, other_ref, total,
    win, xh, xl, fa, fb, grad,
):
    size = probe.shape[1]
    half = size // 2
    steps = half // BLOCK
    count = facts[0, COUNT]

    total[...] = jnp.zeros_like(total)
    grad[...] = jnp.zeros_like(grad)

    def keep(b, which, place, value):
        high, low = split2(value)
        xh[(b, which, *place)] = high
        xl[(b, which, *place)] = low

    def by_right(b, which, table):
        high = xh[b, which]
        x = jnp.concatenate([high, xl[b, which], high], axis=1)
        t = tables[table, 0]
        t = jnp.concatenate([t, t, tables[table, 1]], axis=0)
        return jnp.dot(x, t, preferred_element_type=jnp.float32)

    def by_left(b, which, table):
        high = xh[b, which]
        x = jnp.concatenate([high, xl[b, which], high], axis=0)
        t = tables[table, 0]
        t = jnp.concatenate([t, t, tables[table, 1]], axis=1)
        return jnp.dot(t, x, preferred_element_type=jnp.float32)

    def cut(b, place):
        start, rest_row, base, rest_col = place

        def into(c):
            def use(i, rows_cut):
                win[b, c, i * BLOCK : (i + 1) * BLOCK, :] = rows_cut

            return use

        for c in (0, 1):
            read_window(
                lambda at, rows: ext[c, pl.ds(start + at, rows), pl.ds(base, 384)],
                size, rest_row, rest_col, into(c),
            )
        for i in range(size // BLOCK):
            row = slice(i * BLOCK, (i + 1) * BLOCK)
            wr, wi = win[b, 0, row, :], win[b, 1, row, :]
            pr, pi = probe[0, row, :], probe[1, row, :]
            er = pr * wr - pi * wi
            ei = pr * wi + pi * wr
            keep(b, 0, (row, slice(0, half)), er[:, :half] + er[:, half:])
            keep(b, 0, (row, slice(half, size)), ei[:, :half] + ei[:, half:])
            keep(b, 1, (row, slice(0, half)), er[:, :half] - er[:, half:])
            keep(b, 1, (row, slice(half, size)), ei[:, :half] - ei[:, half:])

    def right_forward(b):
        fa[b] = by_right(b, 0, 1)
        fb[b] = by_right(b, 1, 3)

    def fold_rows(b):
        for i in range(steps):
            top = slice(i * BLOCK, (i + 1) * BLOCK)
            low = slice(half + i * BLOCK, half + (i + 1) * BLOCK)
            for ref, out in ((fa, slice(0, half)), (fb, slice(half, size))):
                t, u = ref[b, top, :], ref[b, low, :]
                s, d = t + u, t - u
                keep(b, 0, (top, out), s[:, :half])
                keep(b, 0, (low, out), s[:, half:])
                keep(b, 1, (top, out), d[:, :half])
                keep(b, 1, (low, out), d[:, half:])

    def left_forward(b):
        fa[b] = by_left(b, 0, 0)
        fb[b] = by_left(b, 1, 2)

    def correct(b, frame, live):
        for i in range(steps):
            top = slice(i * BLOCK, (i + 1) * BLOCK)
            low = slice(half + i * BLOCK, half + (i + 1) * BLOCK)
            for which, ref in ((0, fa), (1, fb)):
                re, im = ref[b, top, :], ref[b, low, :]
                a = amp[frame, pl.ds(which * half + i * BLOCK, BLOCK), :]
                factor = 1.0 - a * lax.rsqrt(re * re + im * im + 0.25)
                factor = jnp.where(live, factor, 0.0)
                keep(b, which, (top, slice(0, size)), re * factor)
                keep(b, which, (low, slice(0, size)), im * factor)

    def left_back(b):
        fa[b] = by_left(b, 0, 1)
        fb[b] = by_left(b, 1, 3)

    def unfold_rows(b):
        for i in range(steps):
            top = slice(i * BLOCK, (i + 1) * BLOCK)
            low = slice(half + i * BLOCK, half + (i + 1) * BLOCK)
            for part, out in ((top, slice(0, half)), (low, slice(half, size))):
                p, q = fa[b, part, :], fb[b, part, :]
                s, d = p + q, p - q
                for place, v in ((top, s), (low, d)):
                    keep(b, 0, (place, out), v[:, :half])
                    keep(b, 1, (place, out), v[:, half:])

    def right_back(b):
        fa[b] = by_right(b, 0, 0)
        fb[b] = by_right(b, 1, 2)

    def spread(b, place):
        start, rest_row, base, rest_col = place
        before = [jnp.zeros((1, 8, 384), jnp.float32)] * 2
        for i in range(size // BLOCK):
            row = slice(i * BLOCK, (i + 1) * BLOCK)
            p, q = fa[b, row, :], fb[b, row, :]
            s, d = p + q, p - q
            br = jnp.concatenate([s[:, :half], d[:, :half]], axis=1)
            bi = jnp.concatenate([s[:, half:], d[:, half:]], axis=1)
            wr, wi = win[b, 0, row, :], win[b, 1, row, :]
            grad[0, row, :] = grad[0, row, :] + (wr * br + wi * bi)
            grad[1, row, :] = grad[1, row, :] + (wr * bi - wi * br)
            pr, pi = probe[0, row, :], probe[1, row, :]
            for c, v in ((0, pr * br + pi * bi), (1, pr * bi - pi * br)):
                part, before[c] = moved_rows(moved_columns(v, rest_col), before[c], rest_row)
                at = (c, pl.ds(start + i * BLOCK, BLOCK), pl.ds(base, 384))
                total[at] = total[at] + part
        for c in (0, 1):
            at = (c, pl.ds(start + size, 8), pl.ds(base, 384))
            total[at] = total[at] + last_rows(before[c], rest_row)

    def two_frames(pair, carry):
        frames = (2 * pair, 2 * pair + 1)
        places = [placed(*corner(facts, 0, frame)) for frame in frames]
        both = (0, 1)
        cut(0, places[0])
        right_forward(0)
        cut(1, places[1])
        right_forward(1)
        for elementwise, product in (
            (lambda b: fold_rows(b), left_forward),
            (lambda b: correct(b, frames[b], frames[b] < count), left_back),
            (lambda b: unfold_rows(b), right_back),
        ):
            for b in both:
                elementwise(b)
                product(b)
        for b in both:
            spread(b, places[b])
        return carry

    lax.fori_loop(0, (count + 1) // 2, two_frames, 0)
    first = facts[0, CORE] == 0
    for i in range(size // BLOCK):
        row = slice(i * BLOCK, (i + 1) * BLOCK)
        re, im = grad[0, row, :], grad[1, row, :]
        mine_ref[row, :] = jnp.where(first, re, im)
        other_ref[row, :] = jnp.where(first, im, re)


def update_kernel(facts, mine_ref, other_ref, probe_ref, out_ref):
    size = mine_ref.shape[0]
    mine, other = mine_ref[...], other_ref[...]
    squares = jnp.sum(mine * mine + other * other)
    step = 0.25 * lax.rsqrt(jnp.full((1, 1), squares / (2 * size * size) + 1e-06, jnp.float32))
    first = facts[0, CORE] == 0
    out_ref[0] = probe_ref[0] - step * jnp.where(first, mine, other)
    out_ref[1] = probe_ref[1] - step * jnp.where(first, other, mine)


def place_of(device):
    region, dev = divmod(device, 64)
    return {
        "x": region // 2,
        "z": (region % 2) * 4 + (dev // 2) % 4,
        "y": dev // 8,
        "core": dev % 2,
    }


def groups_along(by_core):
    groups = {}
    for device in range(512):
        place = place_of(device)
        key = tuple(v for k, v in place.items() if k not in by_core[place["core"]])
        groups.setdefault((place["core"], key), []).append(device)
    return list(groups.values())


def exchanged(parts, names):
    return lax.all_to_all(parts, AXES, 0, 0, tiled=True, axis_index_groups=groups_along(names))


def copies(part, names):
    peers = len(groups_along(names)[0])
    return exchanged(jnp.broadcast_to(part[None], (peers, *part.shape)), names)


def on_device(object_field, probe, amplitudes, row_offset, col_offset, frame_count):
    band, width = object_field.shape[1:]
    size = probe.shape[1]
    slots = amplitudes.shape[2]
    smem = pl.BlockSpec(memory_space=pltpu.SMEM)
    vmem = pl.BlockSpec(memory_space=pltpu.VMEM)
    hbm = pl.BlockSpec(memory_space=pltpu.HBM)
    f32 = jnp.float32
    peers = lax.axis_size("dev")

    rim = lax.ppermute(object_field, "dev", [(i, i - 1) for i in range(1, peers)])
    core = (lax.axis_index("dev") % 2).astype(jnp.int32)
    facts = jnp.concatenate([row_offset[0, 0], col_offset[0, 0], frame_count[0], core[None]])
    facts_before = lax.ppermute(facts, "dev", [(i, i + 1) for i in range(peers - 1)])
    facts = jnp.stack([facts, facts_before])

    ordered, scale = pl.pallas_call(
        prepare_kernel,
        out_shape=(
            jax.ShapeDtypeStruct((slots, size, size), f32),
            jax.ShapeDtypeStruct((band, width), f32),
        ),
        in_specs=[smem, vmem, vmem, vmem],
        out_specs=(vmem, vmem),
        scratch_shapes=[
            pltpu.VMEM((2 * band + size, width), f32),
            pltpu.VMEM((size, size // 2), f32),
        ],
        compiler_params=pltpu.CompilerParams(vmem_limit_bytes=24000 * 1024),
        cost_estimate=pl.CostEstimate(flops=800_000_000, bytes_accessed=3_200_000, transcendentals=0),
        name="prepare",
    )(facts, amplitudes[0, 0], probe, jnp.asarray(order_table(size)))

    bf16 = jnp.bfloat16
    ext = jnp.pad(object_field, ((0, 0), (0, size), (0, 0)))
    ext, rim = lax.optimization_barrier((ext, rim))
    ext = lax.dynamic_update_slice(ext, rim[:, :size], (0, band, 0))
    mine, other, total = pl.pallas_call(
        frames_kernel,
        out_shape=(
            jax.ShapeDtypeStruct((size, size), f32),
            jax.ShapeDtypeStruct((size, size), f32),
            jax.ShapeDtypeStruct((2, band + size, width), f32),
        ),
        in_specs=[smem, vmem, vmem, vmem, vmem],
        out_specs=(vmem, vmem, vmem),
        scratch_shapes=[
            pltpu.VMEM((2, 2, size, size), f32),
            pltpu.VMEM((2, 2, size, size), bf16),
            pltpu.VMEM((2, 2, size, size), bf16),
            pltpu.VMEM((2, size, size), f32),
            pltpu.VMEM((2, size, size), f32),
            pltpu.VMEM((2, size, size), f32),
        ],
        compiler_params=pltpu.CompilerParams(vmem_limit_bytes=24 * 1024 * 1024),
        cost_estimate=pl.CostEstimate(flops=3_300_000_000, bytes_accessed=8_000_000, transcendentals=262144),
        name="frames",
    )(facts, ext, probe, ordered, jnp.asarray(frame_tables(size)))
    over = total[:, band:]
    steps = [(i, i + 1) for i in range(peers - 1)]
    swap = [(i, i ^ 1) for i in range(peers)]
    plane = mine + lax.ppermute(other, "dev", swap)
    incoming = lax.ppermute(over, "dev", steps)
    parts = exchanged(plane.reshape(32, size // 32, size), WIDE)
    share = jnp.sum(parts, axis=0)
    share = jnp.sum(copies(share, LINE), axis=0)
    share, incoming = lax.optimization_barrier((share, incoming))
    plane = copies(share, WIDE).reshape(size, size)
    plane, total = lax.optimization_barrier((plane, total))
    plane_other = lax.ppermute(plane, "dev", swap)
    own = total[:, :band]
    new_field = object_field - jnp.concatenate(
        [own[:, :size] + incoming, own[:, size:]], axis=1
    ) * scale[None]

    new_probe = pl.pallas_call(
        update_kernel,
        out_shape=jax.ShapeDtypeStruct(probe.shape, f32),
        in_specs=[smem, vmem, vmem, vmem],
        out_specs=vmem,
        compiler_params=pltpu.CompilerParams(vmem_limit_bytes=8 * 1024 * 1024),
        cost_estimate=pl.CostEstimate(flops=1_000_000, bytes_accessed=1_600_000, transcendentals=1),
        name="update",
    )(facts, plane, plane_other, probe)
    return (new_field, new_probe)


def solution(mesh):
    return jax.shard_map(
        on_device,
        mesh=mesh,
        in_specs=(
            P(None, ("region", "dev"), None),
            P(),
            P("region", "dev", None, None, None),
            P("region", "dev", None),
            P("region", "dev", None),
            P("region", "dev"),
        ),
        out_specs=(P(None, ("region", "dev"), None), P()),
        check_vma=False,
    )
```

```python
import numpy as np
import ml_dtypes

import jax
import jax.numpy as jnp
from jax import lax
from jax.experimental import pallas as pl
from jax.experimental.pallas import tpu as pltpu
from jax.sharding import PartitionSpec as P

AXES = ("region", "dev")
SLOTS = 4
COUNT, CORE = 2 * SLOTS, 2 * SLOTS + 1
BLOCK = 32
WIDE = (("x_lo", "z"), ("x_lo", "y"))
LINE = (("x_hi", "y"), ("x_hi", "z"))


def in_two(table):
    high = table.astype(ml_dtypes.bfloat16)
    low = (table - high.astype(np.float64)).astype(ml_dtypes.bfloat16)
    return high, low


def half_tables(length):
    half = length // 2
    k = np.arange(half)[:, None]
    n = np.arange(half)[None, :]
    forms = []
    for shift in (0, 1):
        turn = (n * (2 * k + shift)) % length
        angle = -2.0 * np.pi * turn / length
        real = np.cos(angle) / np.sqrt(length)
        imag = np.sin(angle) / np.sqrt(length)
        forms.append(np.block([[real, -imag], [imag, real]]))
    return forms


def frame_tables(length):
    first, second = half_tables(length)
    parts = [in_two(form) for form in (first, first.T, second, second.T)]
    return np.stack([np.stack(pair) for pair in parts])


def order_table(length):
    half = length // 2
    table = np.zeros((length, length), np.float32)
    table[2 * np.arange(half), np.arange(half)] = 1.0
    table[2 * np.arange(half) + 1, half + np.arange(half)] = 1.0
    return table.astype(ml_dtypes.bfloat16)


def split2(x):
    high = x.astype(jnp.bfloat16)
    low = (x - high.astype(jnp.float32)).astype(jnp.bfloat16)
    return high, low


def placed(row, col):
    block = jnp.minimum(col // 128, 1)
    return (
        pl.multiple_of(row // 8 * 8, 8),
        row % 8,
        pl.multiple_of(block * 128, 128),
        col - block * 128,
    )


def corner(facts, source, frame):
    return facts[source, frame], facts[source, SLOTS + frame]


def tiles(x):
    return x.reshape(x.shape[0] // 8, 8, x.shape[1])


def cut_columns(x, rest):
    shift = (128 - rest) & 127
    r = [pltpu.roll(x[:, 128 * j : 128 * j + 128], shift, axis=1) for j in range(3)]
    inside = lax.broadcasted_iota(jnp.int32, r[0].shape, 1) < 128 - rest
    return jnp.concatenate([jnp.where(inside, r[0], r[1]), jnp.where(inside, r[1], r[2])], axis=1)


def turned(x, shift):
    return pltpu.roll(tiles(x), shift & 7, axis=1)


def read_window(read, size, rest_row, rest_col, use):
    after = turned(cut_columns(read(size, 8), rest_col), 8 - rest_row)
    for i in reversed(range(size // BLOCK)):
        here = turned(cut_columns(read(i * BLOCK, BLOCK), rest_col), 8 - rest_row)
        later = jnp.concatenate([here[1:], after], axis=0)
        sub = lax.broadcasted_iota(jnp.int32, here.shape, 1)
        use(i, jnp.where(sub < 8 - rest_row, here, later).reshape(BLOCK, -1))
        after = here[:1]


def moved_columns(x, rest):
    shift = rest & 127
    ra = pltpu.roll(x[:, :128], shift, axis=1)
    rb = pltpu.roll(x[:, 128:], shift, axis=1)
    inside = lax.broadcasted_iota(jnp.int32, ra.shape, 1) >= rest
    zero = jnp.zeros_like(ra)
    return jnp.concatenate(
        [jnp.where(inside, ra, zero), jnp.where(inside, rb, ra), jnp.where(inside, zero, rb)], axis=1
    )


def moved_rows(x, before, rest_row):
    here = turned(x, rest_row)
    earlier = jnp.concatenate([before, here[:-1]], axis=0)
    sub = lax.broadcasted_iota(jnp.int32, here.shape, 1)
    return jnp.where(sub >= rest_row, here, earlier).reshape(x.shape), here[-1:]


def last_rows(before, rest_row):
    sub = lax.broadcasted_iota(jnp.int32, before.shape, 1)
    return jnp.where(sub >= rest_row, 0.0, before).reshape(8, -1)


def prepare_kernel(facts, amp_ref, probe_ref, order_ref, out_ref, weight_ref, total, side):
    band = weight_ref.shape[0]
    size = probe_ref.shape[1]
    half = size // 2
    total[...] = jnp.zeros_like(total)

    def add_power(source, frame, down):
        start, rest_row, base, rest_col = placed(*corner(facts, source, frame))
        before = jnp.zeros((1, 8, 384), jnp.float32)
        for i in range(size // BLOCK):
            pr = probe_ref[0, i * BLOCK : (i + 1) * BLOCK, :]
            pi = probe_ref[1, i * BLOCK : (i + 1) * BLOCK, :]
            part, before = moved_rows(moved_columns(pr * pr + pi * pi, rest_col), before, rest_row)
            place = (pl.ds(start + (down + i * BLOCK), BLOCK), pl.ds(base, 384))
            total[place] = total[place] + part
        place = (pl.ds(start + (down + size), 8), pl.ds(base, 384))
        total[place] = total[place] + last_rows(before, rest_row)

    def own(frame, carry):
        add_power(0, frame, band)
        return carry

    def previous(frame, carry):
        add_power(1, frame, 0)
        return carry

    lax.fori_loop(0, facts[0, COUNT], own, 0)
    lax.fori_loop(0, facts[1, COUNT], previous, 0)
    for i in range(band // BLOCK):
        weight_ref[i * BLOCK : (i + 1) * BLOCK, :] = 1.0 / (
            total[band + i * BLOCK : band + (i + 1) * BLOCK, :] + 1.0
        )

    def permute(frame, carry):
        x = amp_ref[frame]
        high = x.astype(jnp.bfloat16)
        left = x - high.astype(jnp.float32)
        mid = left.astype(jnp.bfloat16)
        low = (left - mid.astype(jnp.float32)).astype(jnp.bfloat16)
        order = order_ref[...]
        y = (
            jnp.dot(high, order, preferred_element_type=jnp.float32)
            + jnp.dot(mid, order, preferred_element_type=jnp.float32)
            + jnp.dot(low, order, preferred_element_type=jnp.float32)
        )
        for j in (0, 1):
            column = slice(j * half, (j + 1) * half)
            side[...] = y[:, column]
            for parity in (0, 1):
                out_ref[frame, parity * half : (parity + 1) * half, column] = side[
                    pl.ds(parity, half, stride=2), :
                ]
        return carry

    lax.fori_loop(0, facts[0, COUNT], permute, 0)


def frames_kernel(
    facts, ext, probe, amp, tables,
    mine_ref, other_ref, total,
    win, xh, xl, fa, fb, grad,
):
    size = probe.shape[1]
    half = size // 2
    steps = half // BLOCK
    count = facts[0, COUNT]

    total[...] = jnp.zeros_like(total)
    grad[...] = jnp.zeros_like(grad)

    def keep(b, which, place, value):
        high, low = split2(value)
        xh[(b, which, *place)] = high
        xl[(b, which, *place)] = low

    def by_right(b, which, table):
        high = xh[b, which]
        x = jnp.concatenate([high, xl[b, which], high], axis=1)
        t = tables[table, 0]
        t = jnp.concatenate([t, t, tables[table, 1]], axis=0)
        return jnp.dot(x, t, preferred_element_type=jnp.float32)

    def by_left(b, which, table):
        high = xh[b, which]
        x = jnp.concatenate([high, xl[b, which], high], axis=0)
        t = tables[table, 0]
        t = jnp.concatenate([t, t, tables[table, 1]], axis=1)
        return jnp.dot(t, x, preferred_element_type=jnp.float32)

    def cut(b, place):
        start, rest_row, base, rest_col = place

        def into(c):
            def use(i, rows_cut):
                win[b, c, i * BLOCK : (i + 1) * BLOCK, :] = rows_cut

            return use

        for c in (0, 1):
            read_window(
                lambda at, rows: ext[c, pl.ds(start + at, rows), pl.ds(base, 384)],
                size, rest_row, rest_col, into(c),
            )
        for i in range(size // BLOCK):
            row = slice(i * BLOCK, (i + 1) * BLOCK)
            wr, wi = win[b, 0, row, :], win[b, 1, row, :]
            pr, pi = probe[0, row, :], probe[1, row, :]
            er = pr * wr - pi * wi
            ei = pr * wi + pi * wr
            keep(b, 0, (row, slice(0, half)), er[:, :half] + er[:, half:])
            keep(b, 0, (row, slice(half, size)), ei[:, :half] + ei[:, half:])
            keep(b, 1, (row, slice(0, half)), er[:, :half] - er[:, half:])
            keep(b, 1, (row, slice(half, size)), ei[:, :half] - ei[:, half:])

    def right_forward(b):
        fa[b] = by_right(b, 0, 1)
        fb[b] = by_right(b, 1, 3)

    def fold_rows(b):
        for i in range(steps):
            top = slice(i * BLOCK, (i + 1) * BLOCK)
            low = slice(half + i * BLOCK, half + (i + 1) * BLOCK)
            for ref, out in ((fa, slice(0, half)), (fb, slice(half, size))):
                t, u = ref[b, top, :], ref[b, low, :]
                s, d = t + u, t - u
                keep(b, 0, (top, out), s[:, :half])
                keep(b, 0, (low, out), s[:, half:])
                keep(b, 1, (top, out), d[:, :half])
                keep(b, 1, (low, out), d[:, half:])

    def left_forward(b):
        fa[b] = by_left(b, 0, 0)
        fb[b] = by_left(b, 1, 2)

    def correct(b, frame, live):
        for i in range(steps):
            top = slice(i * BLOCK, (i + 1) * BLOCK)
            low = slice(half + i * BLOCK, half + (i + 1) * BLOCK)
            for which, ref in ((0, fa), (1, fb)):
                re, im = ref[b, top, :], ref[b, low, :]
                a = amp[frame, pl.ds(which * half + i * BLOCK, BLOCK), :]
                factor = 1.0 - a * lax.rsqrt(re * re + im * im + 0.25)
                factor = jnp.where(live, factor, 0.0)
                keep(b, which, (top, slice(0, size)), re * factor)
                keep(b, which, (low, slice(0, size)), im * factor)

    def left_back(b):
        fa[b] = by_left(b, 0, 1)
        fb[b] = by_left(b, 1, 3)

    def unfold_rows(b):
        for i in range(steps):
            top = slice(i * BLOCK, (i + 1) * BLOCK)
            low = slice(half + i * BLOCK, half + (i + 1) * BLOCK)
            for part, out in ((top, slice(0, half)), (low, slice(half, size))):
                p, q = fa[b, part, :], fb[b, part, :]
                s, d = p + q, p - q
                for place, v in ((top, s), (low, d)):
                    keep(b, 0, (place, out), v[:, :half])
                    keep(b, 1, (place, out), v[:, half:])

    def right_back(b):
        fa[b] = by_right(b, 0, 0)
        fb[b] = by_right(b, 1, 2)

    def spread(b, place):
        start, rest_row, base, rest_col = place
        before = [jnp.zeros((1, 8, 384), jnp.float32)] * 2
        for i in range(size // BLOCK):
            row = slice(i * BLOCK, (i + 1) * BLOCK)
            p, q = fa[b, row, :], fb[b, row, :]
            s, d = p + q, p - q
            br = jnp.concatenate([s[:, :half], d[:, :half]], axis=1)
            bi = jnp.concatenate([s[:, half:], d[:, half:]], axis=1)
            wr, wi = win[b, 0, row, :], win[b, 1, row, :]
            grad[0, row, :] = grad[0, row, :] + (wr * br + wi * bi)
            grad[1, row, :] = grad[1, row, :] + (wr * bi - wi * br)
            pr, pi = probe[0, row, :], probe[1, row, :]
            for c, v in ((0, pr * br + pi * bi), (1, pr * bi - pi * br)):
                part, before[c] = moved_rows(moved_columns(v, rest_col), before[c], rest_row)
                at = (c, pl.ds(start + i * BLOCK, BLOCK), pl.ds(base, 384))
                total[at] = total[at] + part
        for c in (0, 1):
            at = (c, pl.ds(start + size, 8), pl.ds(base, 384))
            total[at] = total[at] + last_rows(before[c], rest_row)

    def two_frames(pair, carry):
        frames = (2 * pair, 2 * pair + 1)
        places = [placed(*corner(facts, 0, frame)) for frame in frames]
        both = (0, 1)
        cut(0, places[0])
        right_forward(0)
        cut(1, places[1])
        right_forward(1)
        for elementwise, product in (
            (lambda b: fold_rows(b), left_forward),
            (lambda b: correct(b, frames[b], frames[b] < count), left_back),
            (lambda b: unfold_rows(b), right_back),
        ):
            for b in both:
                elementwise(b)
                product(b)
        for b in both:
            spread(b, places[b])
        return carry

    lax.fori_loop(0, (count + 1) // 2, two_frames, 0)
    first = facts[0, CORE] == 0
    for i in range(size // BLOCK):
        row = slice(i * BLOCK, (i + 1) * BLOCK)
        re, im = grad[0, row, :], grad[1, row, :]
        mine_ref[row, :] = jnp.where(first, re, im)
        other_ref[row, :] = jnp.where(first, im, re)


def update_kernel(facts, mine_ref, other_ref, probe_ref, out_ref):
    size = mine_ref.shape[0]
    mine, other = mine_ref[...], other_ref[...]
    squares = jnp.sum(mine * mine + other * other)
    step = 0.25 * lax.rsqrt(jnp.full((1, 1), squares / (2 * size * size) + 1e-06, jnp.float32))
    first = facts[0, CORE] == 0
    out_ref[0] = probe_ref[0] - step * jnp.where(first, mine, other)
    out_ref[1] = probe_ref[1] - step * jnp.where(first, other, mine)


def place_of(device):
    region, dev = divmod(device, 64)
    return {
        "x_hi": region // 4,
        "x_lo": region // 2 % 2,
        "z": (region % 2) * 4 + (dev // 2) % 4,
        "y": dev // 8,
        "core": dev % 2,
    }


def groups_along(by_core):
    groups = {}
    for device in range(512):
        place = place_of(device)
        key = tuple(v for k, v in place.items() if k not in by_core[place["core"]])
        groups.setdefault((place["core"], key), []).append(device)
    return list(groups.values())


def exchanged(parts, names):
    return lax.all_to_all(parts, AXES, 0, 0, tiled=True, axis_index_groups=groups_along(names))


def copies(part, names):
    peers = len(groups_along(names)[0])
    return exchanged(jnp.broadcast_to(part[None], (peers, *part.shape)), names)


def on_device(object_field, probe, amplitudes, row_offset, col_offset, frame_count):
    band, width = object_field.shape[1:]
    size = probe.shape[1]
    slots = amplitudes.shape[2]
    smem = pl.BlockSpec(memory_space=pltpu.SMEM)
    vmem = pl.BlockSpec(memory_space=pltpu.VMEM)
    hbm = pl.BlockSpec(memory_space=pltpu.HBM)
    f32 = jnp.float32
    peers = lax.axis_size("dev")

    rim = lax.ppermute(object_field, "dev", [(i, i - 1) for i in range(1, peers)])
    core = (lax.axis_index("dev") % 2).astype(jnp.int32)
    facts = jnp.concatenate([row_offset[0, 0], col_offset[0, 0], frame_count[0], core[None]])
    facts_before = lax.ppermute(facts, "dev", [(i, i + 1) for i in range(peers - 1)])
    facts = jnp.stack([facts, facts_before])

    ordered, scale = pl.pallas_call(
        prepare_kernel,
        out_shape=(
            jax.ShapeDtypeStruct((slots, size, size), f32),
            jax.ShapeDtypeStruct((band, width), f32),
        ),
        in_specs=[smem, vmem, vmem, vmem],
        out_specs=(vmem, vmem),
        scratch_shapes=[
            pltpu.VMEM((2 * band + size, width), f32),
            pltpu.VMEM((size, size // 2), f32),
        ],
        compiler_params=pltpu.CompilerParams(vmem_limit_bytes=24000 * 1024),
        cost_estimate=pl.CostEstimate(flops=800_000_000, bytes_accessed=3_200_000, transcendentals=0),
        name="prepare",
    )(facts, amplitudes[0, 0], probe, jnp.asarray(order_table(size)))

    bf16 = jnp.bfloat16
    ext = jnp.pad(object_field, ((0, 0), (0, size), (0, 0)))
    ext, rim = lax.optimization_barrier((ext, rim))
    ext = lax.dynamic_update_slice(ext, rim[:, :size], (0, band, 0))
    mine, other, total = pl.pallas_call(
        frames_kernel,
        out_shape=(
            jax.ShapeDtypeStruct((size, size), f32),
            jax.ShapeDtypeStruct((size, size), f32),
            jax.ShapeDtypeStruct((2, band + size, width), f32),
        ),
        in_specs=[smem, vmem, vmem, vmem, vmem],
        out_specs=(vmem, vmem, vmem),
        scratch_shapes=[
            pltpu.VMEM((2, 2, size, size), f32),
            pltpu.VMEM((2, 2, size, size), bf16),
            pltpu.VMEM((2, 2, size, size), bf16),
            pltpu.VMEM((2, size, size), f32),
            pltpu.VMEM((2, size, size), f32),
            pltpu.VMEM((2, size, size), f32),
        ],
        compiler_params=pltpu.CompilerParams(vmem_limit_bytes=24 * 1024 * 1024),
        cost_estimate=pl.CostEstimate(flops=3_300_000_000, bytes_accessed=8_000_000, transcendentals=262144),
        name="frames",
    )(facts, ext, probe, ordered, jnp.asarray(frame_tables(size)))
    over = total[:, band:]
    steps = [(i, i + 1) for i in range(peers - 1)]
    swap = [(i, i ^ 1) for i in range(peers)]
    plane = mine + lax.ppermute(other, "dev", swap)
    incoming = lax.ppermute(over, "dev", steps)
    parts = exchanged(plane.reshape(16, size // 16, size), WIDE)
    share = jnp.sum(parts, axis=0)
    share = jnp.sum(copies(share, LINE), axis=0)
    share, total = lax.optimization_barrier((share, total))
    own = total[:, :band]
    new_field = object_field - jnp.concatenate(
        [own[:, :size] + incoming, own[:, size:]], axis=1
    ) * scale[None]
    plane = copies(share, WIDE).reshape(size, size)
    plane, new_field = lax.optimization_barrier((plane, new_field))
    plane_other = lax.ppermute(plane, "dev", swap)

    new_probe = pl.pallas_call(
        update_kernel,
        out_shape=jax.ShapeDtypeStruct(probe.shape, f32),
        in_specs=[smem, vmem, vmem, vmem],
        out_specs=vmem,
        compiler_params=pltpu.CompilerParams(vmem_limit_bytes=8 * 1024 * 1024),
        cost_estimate=pl.CostEstimate(flops=1_000_000, bytes_accessed=1_600_000, transcendentals=1),
        name="update",
    )(facts, plane, plane_other, probe)
    return (new_field, new_probe)


def solution(mesh):
    return jax.shard_map(
        on_device,
        mesh=mesh,
        in_specs=(
            P(None, ("region", "dev"), None),
            P(),
            P("region", "dev", None, None, None),
            P("region", "dev", None),
            P("region", "dev", None),
            P("region", "dev"),
        ),
        out_specs=(P(None, ("region", "dev"), None), P()),
        check_vma=False,
    )
```

```python
import numpy as np
import ml_dtypes

import jax
import jax.numpy as jnp
from jax import lax
from jax.experimental import pallas as pl
from jax.experimental.pallas import tpu as pltpu
from jax.sharding import PartitionSpec as P

AXES = ("region", "dev")
SLOTS = 4
COUNT, CORE = 2 * SLOTS, 2 * SLOTS + 1
BLOCK = 32
WIDE = (("x_lo", "z"), ("x_lo", "y"))
LINE = (("x_hi", "y"), ("x_hi", "z"))


def in_two(table):
    high = table.astype(ml_dtypes.bfloat16)
    low = (table - high.astype(np.float64)).astype(ml_dtypes.bfloat16)
    return high, low


def half_tables(length):
    half = length // 2
    k = np.arange(half)[:, None]
    n = np.arange(half)[None, :]
    forms = []
    for shift in (0, 1):
        turn = (n * (2 * k + shift)) % length
        angle = -2.0 * np.pi * turn / length
        real = np.cos(angle) / np.sqrt(length)
        imag = np.sin(angle) / np.sqrt(length)
        forms.append(np.block([[real, -imag], [imag, real]]))
    return forms


def frame_tables(length):
    first, second = half_tables(length)
    parts = [in_two(form) for form in (first, first.T, second, second.T)]
    return np.stack([np.stack(pair) for pair in parts])


def order_table(length):
    half = length // 2
    table = np.zeros((length, length), np.float32)
    table[2 * np.arange(half), np.arange(half)] = 1.0
    table[2 * np.arange(half) + 1, half + np.arange(half)] = 1.0
    return table.astype(ml_dtypes.bfloat16)


def split2(x):
    high = x.astype(jnp.bfloat16)
    low = (x - high.astype(jnp.float32)).astype(jnp.bfloat16)
    return high, low


def placed(row, col):
    block = jnp.minimum(col // 128, 1)
    return (
        pl.multiple_of(row // 8 * 8, 8),
        row % 8,
        pl.multiple_of(block * 128, 128),
        col - block * 128,
    )


def corner(facts, source, frame):
    return facts[source, frame], facts[source, SLOTS + frame]


def tiles(x):
    return x.reshape(x.shape[0] // 8, 8, x.shape[1])


def cut_columns(x, rest):
    shift = (128 - rest) & 127
    r = [pltpu.roll(x[:, 128 * j : 128 * j + 128], shift, axis=1) for j in range(3)]
    inside = lax.broadcasted_iota(jnp.int32, r[0].shape, 1) < 128 - rest
    return jnp.concatenate([jnp.where(inside, r[0], r[1]), jnp.where(inside, r[1], r[2])], axis=1)


def turned(x, shift):
    return pltpu.roll(tiles(x), shift & 7, axis=1)


def read_window(read, size, rest_row, rest_col, use):
    after = turned(cut_columns(read(size, 8), rest_col), 8 - rest_row)
    for i in reversed(range(size // BLOCK)):
        here = turned(cut_columns(read(i * BLOCK, BLOCK), rest_col), 8 - rest_row)
        later = jnp.concatenate([here[1:], after], axis=0)
        sub = lax.broadcasted_iota(jnp.int32, here.shape, 1)
        use(i, jnp.where(sub < 8 - rest_row, here, later).reshape(BLOCK, -1))
        after = here[:1]


def moved_columns(x, rest):
    shift = rest & 127
    ra = pltpu.roll(x[:, :128], shift, axis=1)
    rb = pltpu.roll(x[:, 128:], shift, axis=1)
    inside = lax.broadcasted_iota(jnp.int32, ra.shape, 1) >= rest
    zero = jnp.zeros_like(ra)
    return jnp.concatenate(
        [jnp.where(inside, ra, zero), jnp.where(inside, rb, ra), jnp.where(inside, zero, rb)], axis=1
    )


def moved_rows(x, before, rest_row):
    here = turned(x, rest_row)
    earlier = jnp.concatenate([before, here[:-1]], axis=0)
    sub = lax.broadcasted_iota(jnp.int32, here.shape, 1)
    return jnp.where(sub >= rest_row, here, earlier).reshape(x.shape), here[-1:]


def last_rows(before, rest_row):
    sub = lax.broadcasted_iota(jnp.int32, before.shape, 1)
    return jnp.where(sub >= rest_row, 0.0, before).reshape(8, -1)


def prepare_kernel(facts, amp_ref, probe_ref, order_ref, out_ref, weight_ref, total, side):
    band = weight_ref.shape[0]
    size = probe_ref.shape[1]
    half = size // 2
    total[...] = jnp.zeros_like(total)

    def add_power(source, frame, down):
        start, rest_row, base, rest_col = placed(*corner(facts, source, frame))
        before = jnp.zeros((1, 8, 384), jnp.float32)
        for i in range(size // BLOCK):
            pr = probe_ref[0, i * BLOCK : (i + 1) * BLOCK, :]
            pi = probe_ref[1, i * BLOCK : (i + 1) * BLOCK, :]
            part, before = moved_rows(moved_columns(pr * pr + pi * pi, rest_col), before, rest_row)
            place = (pl.ds(start + (down + i * BLOCK), BLOCK), pl.ds(base, 384))
            total[place] = total[place] + part
        place = (pl.ds(start + (down + size), 8), pl.ds(base, 384))
        total[place] = total[place] + last_rows(before, rest_row)

    def own(frame, carry):
        add_power(0, frame, band)
        return carry

    def previous(frame, carry):
        add_power(1, frame, 0)
        return carry

    lax.fori_loop(0, facts[0, COUNT], own, 0)
    lax.fori_loop(0, facts[1, COUNT], previous, 0)
    for i in range(band // BLOCK):
        weight_ref[i * BLOCK : (i + 1) * BLOCK, :] = 1.0 / (
            total[band + i * BLOCK : band + (i + 1) * BLOCK, :] + 1.0
        )

    def permute(frame, carry):
        x = amp_ref[frame]
        high = x.astype(jnp.bfloat16)
        left = x - high.astype(jnp.float32)
        mid = left.astype(jnp.bfloat16)
        low = (left - mid.astype(jnp.float32)).astype(jnp.bfloat16)
        order = order_ref[...]
        y = (
            jnp.dot(high, order, preferred_element_type=jnp.float32)
            + jnp.dot(mid, order, preferred_element_type=jnp.float32)
            + jnp.dot(low, order, preferred_element_type=jnp.float32)
        )
        for j in (0, 1):
            column = slice(j * half, (j + 1) * half)
            side[...] = y[:, column]
            for parity in (0, 1):
                out_ref[frame, parity * half : (parity + 1) * half, column] = side[
                    pl.ds(parity, half, stride=2), :
                ]
        return carry

    lax.fori_loop(0, facts[0, COUNT], permute, 0)


def frames_kernel(
    facts, ext, probe, amp, tables,
    mine_ref, other_ref, total,
    win, xh, xl, fa, fb, grad,
):
    size = probe.shape[1]
    half = size // 2
    steps = half // BLOCK
    count = facts[0, COUNT]

    total[...] = jnp.zeros_like(total)
    grad[...] = jnp.zeros_like(grad)

    def keep(b, which, place, value):
        high, low = split2(value)
        xh[(b, which, *place)] = high
        xl[(b, which, *place)] = low

    def by_right(b, which, table):
        high = xh[b, which]
        x = jnp.concatenate([high, xl[b, which], high], axis=1)
        t = tables[table, 0]
        t = jnp.concatenate([t, t, tables[table, 1]], axis=0)
        return jnp.dot(x, t, preferred_element_type=jnp.float32)

    def by_left(b, which, table):
        high = xh[b, which]
        x = jnp.concatenate([high, xl[b, which], high], axis=0)
        t = tables[table, 0]
        t = jnp.concatenate([t, t, tables[table, 1]], axis=1)
        return jnp.dot(t, x, preferred_element_type=jnp.float32)

    def cut(b, place):
        start, rest_row, base, rest_col = place

        def into(c):
            def use(i, rows_cut):
                win[b, c, i * BLOCK : (i + 1) * BLOCK, :] = rows_cut

            return use

        for c in (0, 1):
            read_window(
                lambda at, rows: ext[c, pl.ds(start + at, rows), pl.ds(base, 384)],
                size, rest_row, rest_col, into(c),
            )
        for i in range(size // BLOCK):
            row = slice(i * BLOCK, (i + 1) * BLOCK)
            wr, wi = win[b, 0, row, :], win[b, 1, row, :]
            pr, pi = probe[0, row, :], probe[1, row, :]
            er = pr * wr - pi * wi
            ei = pr * wi + pi * wr
            keep(b, 0, (row, slice(0, half)), er[:, :half] + er[:, half:])
            keep(b, 0, (row, slice(half, size)), ei[:, :half] + ei[:, half:])
            keep(b, 1, (row, slice(0, half)), er[:, :half] - er[:, half:])
            keep(b, 1, (row, slice(half, size)), ei[:, :half] - ei[:, half:])

    def right_forward(b):
        fa[b] = by_right(b, 0, 1)
        fb[b] = by_right(b, 1, 3)

    def fold_rows(b):
        for i in range(steps):
            top = slice(i * BLOCK, (i + 1) * BLOCK)
            low = slice(half + i * BLOCK, half + (i + 1) * BLOCK)
            for ref, out in ((fa, slice(0, half)), (fb, slice(half, size))):
                t, u = ref[b, top, :], ref[b, low, :]
                s, d = t + u, t - u
                keep(b, 0, (top, out), s[:, :half])
                keep(b, 0, (low, out), s[:, half:])
                keep(b, 1, (top, out), d[:, :half])
                keep(b, 1, (low, out), d[:, half:])

    def left_forward(b):
        fa[b] = by_left(b, 0, 0)
        fb[b] = by_left(b, 1, 2)

    def correct(b, frame, live):
        for i in range(steps):
            top = slice(i * BLOCK, (i + 1) * BLOCK)
            low = slice(half + i * BLOCK, half + (i + 1) * BLOCK)
            for which, ref in ((0, fa), (1, fb)):
                re, im = ref[b, top, :], ref[b, low, :]
                a = amp[frame, pl.ds(which * half + i * BLOCK, BLOCK), :]
                factor = 1.0 - a * lax.rsqrt(re * re + im * im + 0.25)
                factor = jnp.where(live, factor, 0.0)
                keep(b, which, (top, slice(0, size)), re * factor)
                keep(b, which, (low, slice(0, size)), im * factor)

    def left_back(b):
        fa[b] = by_left(b, 0, 1)
        fb[b] = by_left(b, 1, 3)

    def unfold_rows(b):
        for i in range(steps):
            top = slice(i * BLOCK, (i + 1) * BLOCK)
            low = slice(half + i * BLOCK, half + (i + 1) * BLOCK)
            for part, out in ((top, slice(0, half)), (low, slice(half, size))):
                p, q = fa[b, part, :], fb[b, part, :]
                s, d = p + q, p - q
                for place, v in ((top, s), (low, d)):
                    keep(b, 0, (place, out), v[:, :half])
                    keep(b, 1, (place, out), v[:, half:])

    def right_back(b):
        fa[b] = by_right(b, 0, 0)
        fb[b] = by_right(b, 1, 2)

    def spread(b, place):
        start, rest_row, base, rest_col = place
        before = [jnp.zeros((1, 8, 384), jnp.float32)] * 2
        for i in range(size // BLOCK):
            row = slice(i * BLOCK, (i + 1) * BLOCK)
            p, q = fa[b, row, :], fb[b, row, :]
            s, d = p + q, p - q
            br = jnp.concatenate([s[:, :half], d[:, :half]], axis=1)
            bi = jnp.concatenate([s[:, half:], d[:, half:]], axis=1)
            wr, wi = win[b, 0, row, :], win[b, 1, row, :]
            grad[0, row, :] = grad[0, row, :] + (wr * br + wi * bi)
            grad[1, row, :] = grad[1, row, :] + (wr * bi - wi * br)
            pr, pi = probe[0, row, :], probe[1, row, :]
            for c, v in ((0, pr * br + pi * bi), (1, pr * bi - pi * br)):
                part, before[c] = moved_rows(moved_columns(v, rest_col), before[c], rest_row)
                at = (c, pl.ds(start + i * BLOCK, BLOCK), pl.ds(base, 384))
                total[at] = total[at] + part
        for c in (0, 1):
            at = (c, pl.ds(start + size, 8), pl.ds(base, 384))
            total[at] = total[at] + last_rows(before[c], rest_row)

    def two_frames(pair, carry):
        frames = (2 * pair, 2 * pair + 1)
        places = [placed(*corner(facts, 0, frame)) for frame in frames]
        both = (0, 1)
        cut(0, places[0])
        right_forward(0)
        cut(1, places[1])
        right_forward(1)
        for elementwise, product in (
            (lambda b: fold_rows(b), left_forward),
            (lambda b: correct(b, frames[b], frames[b] < count), left_back),
            (lambda b: unfold_rows(b), right_back),
        ):
            for b in both:
                elementwise(b)
                product(b)
        for b in both:
            spread(b, places[b])
        return carry

    lax.fori_loop(0, (count + 1) // 2, two_frames, 0)
    first = facts[0, CORE] == 0
    for i in range(size // BLOCK):
        row = slice(i * BLOCK, (i + 1) * BLOCK)
        re, im = grad[0, row, :], grad[1, row, :]
        mine_ref[row, :] = jnp.where(first, re, im)
        other_ref[row, :] = jnp.where(first, im, re)


def update_kernel(facts, mine_ref, other_ref, probe_ref, out_ref):
    size = mine_ref.shape[0]
    mine, other = mine_ref[...], other_ref[...]
    squares = jnp.sum(mine * mine + other * other)
    step = 0.25 * lax.rsqrt(jnp.full((1, 1), squares / (2 * size * size) + 1e-06, jnp.float32))
    first = facts[0, CORE] == 0
    out_ref[0] = probe_ref[0] - step * jnp.where(first, mine, other)
    out_ref[1] = probe_ref[1] - step * jnp.where(first, other, mine)


def place_of(device):
    region, dev = divmod(device, 64)
    return {
        "x_hi": region // 4,
        "x_lo": region // 2 % 2,
        "z": (region % 2) * 4 + (dev // 2) % 4,
        "y": dev // 8,
        "core": dev % 2,
    }


def groups_along(by_core):
    groups = {}
    for device in range(512):
        place = place_of(device)
        key = tuple(v for k, v in place.items() if k not in by_core[place["core"]])
        groups.setdefault((place["core"], key), []).append(device)
    return list(groups.values())


def exchanged(parts, names):
    return lax.all_to_all(parts, AXES, 0, 0, tiled=True, axis_index_groups=groups_along(names))


def copies(part, names):
    peers = len(groups_along(names)[0])
    return exchanged(jnp.broadcast_to(part[None], (peers, *part.shape)), names)


def on_device(object_field, probe, amplitudes, row_offset, col_offset, frame_count):
    band, width = object_field.shape[1:]
    size = probe.shape[1]
    slots = amplitudes.shape[2]
    smem = pl.BlockSpec(memory_space=pltpu.SMEM)
    vmem = pl.BlockSpec(memory_space=pltpu.VMEM)
    hbm = pl.BlockSpec(memory_space=pltpu.HBM)
    f32 = jnp.float32
    peers = lax.axis_size("dev")

    rim = lax.ppermute(object_field, "dev", [(i, i - 1) for i in range(1, peers)])
    core = (lax.axis_index("dev") % 2).astype(jnp.int32)
    facts = jnp.concatenate([row_offset[0, 0], col_offset[0, 0], frame_count[0], core[None]])
    facts_before = lax.ppermute(facts, "dev", [(i, i + 1) for i in range(peers - 1)])
    facts = jnp.stack([facts, facts_before])

    ordered, scale = pl.pallas_call(
        prepare_kernel,
        out_shape=(
            jax.ShapeDtypeStruct((slots, size, size), f32),
            jax.ShapeDtypeStruct((band, width), f32),
        ),
        in_specs=[smem, vmem, vmem, vmem],
        out_specs=(vmem, vmem),
        scratch_shapes=[
            pltpu.VMEM((2 * band + size, width), f32),
            pltpu.VMEM((size, size // 2), f32),
        ],
        compiler_params=pltpu.CompilerParams(vmem_limit_bytes=24000 * 1024),
        cost_estimate=pl.CostEstimate(flops=800_000_000, bytes_accessed=3_200_000, transcendentals=0),
        name="prepare",
    )(facts, amplitudes[0, 0], probe, jnp.asarray(order_table(size)))

    bf16 = jnp.bfloat16
    ext = jnp.pad(object_field, ((0, 0), (0, size), (0, 0)))
    ext, rim = lax.optimization_barrier((ext, rim))
    ext = lax.dynamic_update_slice(ext, rim[:, :size], (0, band, 0))
    mine, other, total = pl.pallas_call(
        frames_kernel,
        out_shape=(
            jax.ShapeDtypeStruct((size, size), f32),
            jax.ShapeDtypeStruct((size, size), f32),
            jax.ShapeDtypeStruct((2, band + size, width), f32),
        ),
        in_specs=[smem, vmem, vmem, vmem, vmem],
        out_specs=(vmem, vmem, vmem),
        scratch_shapes=[
            pltpu.VMEM((2, 2, size, size), f32),
            pltpu.VMEM((2, 2, size, size), bf16),
            pltpu.VMEM((2, 2, size, size), bf16),
            pltpu.VMEM((2, size, size), f32),
            pltpu.VMEM((2, size, size), f32),
            pltpu.VMEM((2, size, size), f32),
        ],
        compiler_params=pltpu.CompilerParams(vmem_limit_bytes=24 * 1024 * 1024),
        cost_estimate=pl.CostEstimate(flops=3_300_000_000, bytes_accessed=8_000_000, transcendentals=262144),
        name="frames",
    )(facts, ext, probe, ordered, jnp.asarray(frame_tables(size)))
    over = total[:, band:]
    steps = [(i, i + 1) for i in range(peers - 1)]
    swap = [(i, i ^ 1) for i in range(peers)]
    plane = mine + lax.ppermute(other, "dev", swap)
    incoming = lax.ppermute(over, "dev", steps)
    parts = exchanged(plane.reshape(16, size // 16, size), WIDE)
    share = jnp.sum(parts, axis=0)
    share = jnp.sum(copies(share, LINE), axis=0)
    share, total, incoming = lax.optimization_barrier((share, total, incoming))
    own = total[:, :band]
    new_field = object_field - jnp.concatenate(
        [own[:, :size] + incoming, own[:, size:]], axis=1
    ) * scale[None]
    plane = copies(share, WIDE).reshape(size, size)
    plane, new_field = lax.optimization_barrier((plane, new_field))
    plane_other = lax.ppermute(plane, "dev", swap)

    new_probe = pl.pallas_call(
        update_kernel,
        out_shape=jax.ShapeDtypeStruct(probe.shape, f32),
        in_specs=[smem, vmem, vmem, vmem],
        out_specs=vmem,
        compiler_params=pltpu.CompilerParams(vmem_limit_bytes=8 * 1024 * 1024),
        cost_estimate=pl.CostEstimate(flops=1_000_000, bytes_accessed=1_600_000, transcendentals=1),
        name="update",
    )(facts, plane, plane_other, probe)
    return (new_field, new_probe)


def solution(mesh):
    return jax.shard_map(
        on_device,
        mesh=mesh,
        in_specs=(
            P(None, ("region", "dev"), None),
            P(),
            P("region", "dev", None, None, None),
            P("region", "dev", None),
            P("region", "dev", None),
            P("region", "dev"),
        ),
        out_specs=(P(None, ("region", "dev"), None), P()),
        check_vma=False,
    )
```

```python
import numpy as np
import ml_dtypes

import jax
import jax.numpy as jnp
from jax import lax
from jax.experimental import pallas as pl
from jax.experimental.pallas import tpu as pltpu
from jax.sharding import PartitionSpec as P

AXES = ("region", "dev")
SLOTS = 4
COUNT, CORE = 2 * SLOTS, 2 * SLOTS + 1
BLOCK = 32
WIDE = (("x_lo", "z"), ("x_lo", "y"))
LINE = (("x_hi", "y"), ("x_hi", "z"))


def in_two(table):
    high = table.astype(ml_dtypes.bfloat16)
    low = (table - high.astype(np.float64)).astype(ml_dtypes.bfloat16)
    return high, low


def half_tables(length):
    half = length // 2
    k = np.arange(half)[:, None]
    n = np.arange(half)[None, :]
    forms = []
    for shift in (0, 1):
        turn = (n * (2 * k + shift)) % length
        angle = -2.0 * np.pi * turn / length
        real = np.cos(angle) / np.sqrt(length)
        imag = np.sin(angle) / np.sqrt(length)
        forms.append(np.block([[real, -imag], [imag, real]]))
    return forms


def frame_tables(length):
    first, second = half_tables(length)
    parts = [in_two(form) for form in (first, first.T, second, second.T)]
    return np.stack([np.stack(pair) for pair in parts])


def order_table(length):
    half = length // 2
    table = np.zeros((length, length), np.float32)
    table[2 * np.arange(half), np.arange(half)] = 1.0
    table[2 * np.arange(half) + 1, half + np.arange(half)] = 1.0
    return table.astype(ml_dtypes.bfloat16)


def split2(x):
    high = x.astype(jnp.bfloat16)
    low = (x - high.astype(jnp.float32)).astype(jnp.bfloat16)
    return high, low


def placed(row, col):
    block = jnp.minimum(col // 128, 1)
    return (
        pl.multiple_of(row // 8 * 8, 8),
        row % 8,
        pl.multiple_of(block * 128, 128),
        col - block * 128,
    )


def corner(facts, source, frame):
    return facts[source, frame], facts[source, SLOTS + frame]


def tiles(x):
    return x.reshape(x.shape[0] // 8, 8, x.shape[1])


def cut_columns(x, rest):
    shift = (128 - rest) & 127
    r = [pltpu.roll(x[:, 128 * j : 128 * j + 128], shift, axis=1) for j in range(3)]
    inside = lax.broadcasted_iota(jnp.int32, r[0].shape, 1) < 128 - rest
    return jnp.concatenate([jnp.where(inside, r[0], r[1]), jnp.where(inside, r[1], r[2])], axis=1)


def turned(x, shift):
    return pltpu.roll(tiles(x), shift & 7, axis=1)


def read_window(read, size, rest_row, rest_col, use):
    after = turned(cut_columns(read(size, 8), rest_col), 8 - rest_row)
    for i in reversed(range(size // BLOCK)):
        here = turned(cut_columns(read(i * BLOCK, BLOCK), rest_col), 8 - rest_row)
        later = jnp.concatenate([here[1:], after], axis=0)
        sub = lax.broadcasted_iota(jnp.int32, here.shape, 1)
        use(i, jnp.where(sub < 8 - rest_row, here, later).reshape(BLOCK, -1))
        after = here[:1]


def moved_columns(x, rest):
    shift = rest & 127
    ra = pltpu.roll(x[:, :128], shift, axis=1)
    rb = pltpu.roll(x[:, 128:], shift, axis=1)
    inside = lax.broadcasted_iota(jnp.int32, ra.shape, 1) >= rest
    zero = jnp.zeros_like(ra)
    return jnp.concatenate(
        [jnp.where(inside, ra, zero), jnp.where(inside, rb, ra), jnp.where(inside, zero, rb)], axis=1
    )


def moved_rows(x, before, rest_row):
    here = turned(x, rest_row)
    earlier = jnp.concatenate([before, here[:-1]], axis=0)
    sub = lax.broadcasted_iota(jnp.int32, here.shape, 1)
    return jnp.where(sub >= rest_row, here, earlier).reshape(x.shape), here[-1:]


def last_rows(before, rest_row):
    sub = lax.broadcasted_iota(jnp.int32, before.shape, 1)
    return jnp.where(sub >= rest_row, 0.0, before).reshape(8, -1)


def prepare_kernel(facts, amp_ref, probe_ref, order_ref, out_ref, weight_ref, total, side):
    band = weight_ref.shape[0]
    size = probe_ref.shape[1]
    half = size // 2
    total[...] = jnp.zeros_like(total)

    def add_power(source, frame, down):
        start, rest_row, base, rest_col = placed(*corner(facts, source, frame))
        before = jnp.zeros((1, 8, 384), jnp.float32)
        for i in range(size // BLOCK):
            pr = probe_ref[0, i * BLOCK : (i + 1) * BLOCK, :]
            pi = probe_ref[1, i * BLOCK : (i + 1) * BLOCK, :]
            part, before = moved_rows(moved_columns(pr * pr + pi * pi, rest_col), before, rest_row)
            place = (pl.ds(start + (down + i * BLOCK), BLOCK), pl.ds(base, 384))
            total[place] = total[place] + part
        place = (pl.ds(start + (down + size), 8), pl.ds(base, 384))
        total[place] = total[place] + last_rows(before, rest_row)

    def own(frame, carry):
        add_power(0, frame, band)
        return carry

    def previous(frame, carry):
        add_power(1, frame, 0)
        return carry

    lax.fori_loop(0, facts[0, COUNT], own, 0)
    lax.fori_loop(0, facts[1, COUNT], previous, 0)
    for i in range(band // BLOCK):
        weight_ref[i * BLOCK : (i + 1) * BLOCK, :] = 1.0 / (
            total[band + i * BLOCK : band + (i + 1) * BLOCK, :] + 1.0
        )

    def permute(frame, carry):
        x = amp_ref[frame]
        high = x.astype(jnp.bfloat16)
        left = x - high.astype(jnp.float32)
        mid = left.astype(jnp.bfloat16)
        low = (left - mid.astype(jnp.float32)).astype(jnp.bfloat16)
        order = order_ref[...]
        y = (
            jnp.dot(high, order, preferred_element_type=jnp.float32)
            + jnp.dot(mid, order, preferred_element_type=jnp.float32)
            + jnp.dot(low, order, preferred_element_type=jnp.float32)
        )
        for j in (0, 1):
            column = slice(j * half, (j + 1) * half)
            side[...] = y[:, column]
            for parity in (0, 1):
                out_ref[frame, parity * half : (parity + 1) * half, column] = side[
                    pl.ds(parity, half, stride=2), :
                ]
        return carry

    lax.fori_loop(0, facts[0, COUNT], permute, 0)


def frames_kernel(
    facts, ext, probe, amp, tables,
    mine_ref, other_ref, total,
    win, xh, xl, fa, fb, grad,
):
    size = probe.shape[1]
    half = size // 2
    steps = half // BLOCK
    count = facts[0, COUNT]

    total[...] = jnp.zeros_like(total)
    grad[...] = jnp.zeros_like(grad)

    def keep(b, which, place, value):
        high, low = split2(value)
        xh[(b, which, *place)] = high
        xl[(b, which, *place)] = low

    def by_right(b, which, table):
        high = xh[b, which]
        x = jnp.concatenate([high, xl[b, which], high], axis=1)
        t = tables[table, 0]
        t = jnp.concatenate([t, t, tables[table, 1]], axis=0)
        return jnp.dot(x, t, preferred_element_type=jnp.float32)

    def by_left(b, which, table):
        high = xh[b, which]
        x = jnp.concatenate([high, xl[b, which], high], axis=0)
        t = tables[table, 0]
        t = jnp.concatenate([t, t, tables[table, 1]], axis=1)
        return jnp.dot(t, x, preferred_element_type=jnp.float32)

    def cut(b, place):
        start, rest_row, base, rest_col = place

        def into(c):
            def use(i, rows_cut):
                win[b, c, i * BLOCK : (i + 1) * BLOCK, :] = rows_cut

            return use

        for c in (0, 1):
            read_window(
                lambda at, rows: ext[c, pl.ds(start + at, rows), pl.ds(base, 384)],
                size, rest_row, rest_col, into(c),
            )
        for i in range(size // BLOCK):
            row = slice(i * BLOCK, (i + 1) * BLOCK)
            wr, wi = win[b, 0, row, :], win[b, 1, row, :]
            pr, pi = probe[0, row, :], probe[1, row, :]
            er = pr * wr - pi * wi
            ei = pr * wi + pi * wr
            keep(b, 0, (row, slice(0, half)), er[:, :half] + er[:, half:])
            keep(b, 0, (row, slice(half, size)), ei[:, :half] + ei[:, half:])
            keep(b, 1, (row, slice(0, half)), er[:, :half] - er[:, half:])
            keep(b, 1, (row, slice(half, size)), ei[:, :half] - ei[:, half:])

    def right_forward(b):
        fa[b] = by_right(b, 0, 1)
        fb[b] = by_right(b, 1, 3)

    def fold_rows(b):
        for i in range(steps):
            top = slice(i * BLOCK, (i + 1) * BLOCK)
            low = slice(half + i * BLOCK, half + (i + 1) * BLOCK)
            for ref, out in ((fa, slice(0, half)), (fb, slice(half, size))):
                t, u = ref[b, top, :], ref[b, low, :]
                s, d = t + u, t - u
                keep(b, 0, (top, out), s[:, :half])
                keep(b, 0, (low, out), s[:, half:])
                keep(b, 1, (top, out), d[:, :half])
                keep(b, 1, (low, out), d[:, half:])

    def left_forward(b):
        fa[b] = by_left(b, 0, 0)
        fb[b] = by_left(b, 1, 2)

    def correct(b, frame, live):
        for i in range(steps):
            top = slice(i * BLOCK, (i + 1) * BLOCK)
            low = slice(half + i * BLOCK, half + (i + 1) * BLOCK)
            for which, ref in ((0, fa), (1, fb)):
                re, im = ref[b, top, :], ref[b, low, :]
                a = amp[frame, pl.ds(which * half + i * BLOCK, BLOCK), :]
                factor = 1.0 - a * lax.rsqrt(re * re + im * im + 0.25)
                factor = jnp.where(live, factor, 0.0)
                keep(b, which, (top, slice(0, size)), re * factor)
                keep(b, which, (low, slice(0, size)), im * factor)

    def left_back(b):
        fa[b] = by_left(b, 0, 1)
        fb[b] = by_left(b, 1, 3)

    def unfold_rows(b):
        for i in range(steps):
            top = slice(i * BLOCK, (i + 1) * BLOCK)
            low = slice(half + i * BLOCK, half + (i + 1) * BLOCK)
            for part, out in ((top, slice(0, half)), (low, slice(half, size))):
                p, q = fa[b, part, :], fb[b, part, :]
                s, d = p + q, p - q
                for place, v in ((top, s), (low, d)):
                    keep(b, 0, (place, out), v[:, :half])
                    keep(b, 1, (place, out), v[:, half:])

    def right_back(b):
        fa[b] = by_right(b, 0, 0)
        fb[b] = by_right(b, 1, 2)

    def spread(b, place):
        start, rest_row, base, rest_col = place
        before = [jnp.zeros((1, 8, 384), jnp.float32)] * 2
        for i in range(size // BLOCK):
            row = slice(i * BLOCK, (i + 1) * BLOCK)
            p, q = fa[b, row, :], fb[b, row, :]
            s, d = p + q, p - q
            br = jnp.concatenate([s[:, :half], d[:, :half]], axis=1)
            bi = jnp.concatenate([s[:, half:], d[:, half:]], axis=1)
            wr, wi = win[b, 0, row, :], win[b, 1, row, :]
            grad[0, row, :] = grad[0, row, :] + (wr * br + wi * bi)
            grad[1, row, :] = grad[1, row, :] + (wr * bi - wi * br)
            pr, pi = probe[0, row, :], probe[1, row, :]
            for c, v in ((0, pr * br + pi * bi), (1, pr * bi - pi * br)):
                part, before[c] = moved_rows(moved_columns(v, rest_col), before[c], rest_row)
                at = (c, pl.ds(start + i * BLOCK, BLOCK), pl.ds(base, 384))
                total[at] = total[at] + part
        for c in (0, 1):
            at = (c, pl.ds(start + size, 8), pl.ds(base, 384))
            total[at] = total[at] + last_rows(before[c], rest_row)

    def two_frames(pair, carry):
        frames = (2 * pair, 2 * pair + 1)
        places = [placed(*corner(facts, 0, frame)) for frame in frames]
        both = (0, 1)
        cut(0, places[0])
        right_forward(0)
        cut(1, places[1])
        right_forward(1)
        for elementwise, product in (
            (lambda b: fold_rows(b), left_forward),
            (lambda b: correct(b, frames[b], frames[b] < count), left_back),
            (lambda b: unfold_rows(b), right_back),
        ):
            for b in both:
                elementwise(b)
                product(b)
        for b in both:
            spread(b, places[b])
        return carry

    lax.fori_loop(0, (count + 1) // 2, two_frames, 0)
    first = facts[0, CORE] == 0
    for i in range(size // BLOCK):
        row = slice(i * BLOCK, (i + 1) * BLOCK)
        re, im = grad[0, row, :], grad[1, row, :]
        mine_ref[row, :] = jnp.where(first, re, im)
        other_ref[row, :] = jnp.where(first, im, re)


def update_kernel(facts, mine_ref, other_ref, probe_ref, out_ref, held, sems):
    size = mine_ref.shape[0]
    total = jnp.zeros((8, size), jnp.float32)
    for i in range(size // 8):
        row = slice(8 * i, 8 * i + 8)
        mine, other = mine_ref[row, :], other_ref[row, :]
        total = total + (mine * mine + other * other)
    squares = jnp.sum(total)
    step = 0.25 * lax.rsqrt(jnp.full((1, 1), squares / (2 * size * size) + 1e-06, jnp.float32))
    first = facts[0, CORE] == 0
    stores = []
    for j in range(2):
        row = slice(j * size // 2, (j + 1) * size // 2)
        mine, other = mine_ref[row, :], other_ref[row, :]
        for c, part in ((0, jnp.where(first, mine, other)), (1, jnp.where(first, other, mine))):
            held[c, row, :] = probe_ref[c, row, :] - step * part
            stores.append(
                pltpu.make_async_copy(held.at[c, row], out_ref.at[c, row], sems.at[2 * j + c])
            )
            stores[-1].start()
    for store in stores:
        store.wait()


def place_of(device):
    region, dev = divmod(device, 64)
    return {
        "x_hi": region // 4,
        "x_lo": region // 2 % 2,
        "z": (region % 2) * 4 + (dev // 2) % 4,
        "y": dev // 8,
        "core": dev % 2,
    }


def groups_along(by_core):
    groups = {}
    for device in range(512):
        place = place_of(device)
        key = tuple(v for k, v in place.items() if k not in by_core[place["core"]])
        groups.setdefault((place["core"], key), []).append(device)
    return list(groups.values())


def exchanged(parts, names):
    return lax.all_to_all(parts, AXES, 0, 0, tiled=True, axis_index_groups=groups_along(names))


def copies(part, names):
    peers = len(groups_along(names)[0])
    return exchanged(jnp.broadcast_to(part[None], (peers, *part.shape)), names)


def on_device(object_field, probe, amplitudes, row_offset, col_offset, frame_count):
    band, width = object_field.shape[1:]
    size = probe.shape[1]
    slots = amplitudes.shape[2]
    smem = pl.BlockSpec(memory_space=pltpu.SMEM)
    vmem = pl.BlockSpec(memory_space=pltpu.VMEM)
    hbm = pl.BlockSpec(memory_space=pltpu.HBM)
    f32 = jnp.float32
    peers = lax.axis_size("dev")

    rim = lax.ppermute(object_field, "dev", [(i, i - 1) for i in range(1, peers)])
    core = (lax.axis_index("dev") % 2).astype(jnp.int32)
    facts = jnp.concatenate([row_offset[0, 0], col_offset[0, 0], frame_count[0], core[None]])
    facts_before = lax.ppermute(facts, "dev", [(i, i + 1) for i in range(peers - 1)])
    facts = jnp.stack([facts, facts_before])

    ordered, scale = pl.pallas_call(
        prepare_kernel,
        out_shape=(
            jax.ShapeDtypeStruct((slots, size, size), f32),
            jax.ShapeDtypeStruct((band, width), f32),
        ),
        in_specs=[smem, vmem, vmem, vmem],
        out_specs=(vmem, vmem),
        scratch_shapes=[
            pltpu.VMEM((2 * band + size, width), f32),
            pltpu.VMEM((size, size // 2), f32),
        ],
        compiler_params=pltpu.CompilerParams(vmem_limit_bytes=24000 * 1024),
        cost_estimate=pl.CostEstimate(flops=800_000_000, bytes_accessed=3_200_000, transcendentals=0),
        name="prepare",
    )(facts, amplitudes[0, 0], probe, jnp.asarray(order_table(size)))

    bf16 = jnp.bfloat16
    ext = jnp.pad(object_field, ((0, 0), (0, size), (0, 0)))
    ext, rim = lax.optimization_barrier((ext, rim))
    ext = lax.dynamic_update_slice(ext, rim[:, :size], (0, band, 0))
    mine, other, total = pl.pallas_call(
        frames_kernel,
        out_shape=(
            jax.ShapeDtypeStruct((size, size), f32),
            jax.ShapeDtypeStruct((size, size), f32),
            jax.ShapeDtypeStruct((2, band + size, width), f32),
        ),
        in_specs=[smem, vmem, vmem, vmem, vmem],
        out_specs=(vmem, vmem, vmem),
        scratch_shapes=[
            pltpu.VMEM((2, 2, size, size), f32),
            pltpu.VMEM((2, 2, size, size), bf16),
            pltpu.VMEM((2, 2, size, size), bf16),
            pltpu.VMEM((2, size, size), f32),
            pltpu.VMEM((2, size, size), f32),
            pltpu.VMEM((2, size, size), f32),
        ],
        compiler_params=pltpu.CompilerParams(vmem_limit_bytes=24 * 1024 * 1024),
        cost_estimate=pl.CostEstimate(flops=3_300_000_000, bytes_accessed=8_000_000, transcendentals=262144),
        name="frames",
    )(facts, ext, probe, ordered, jnp.asarray(frame_tables(size)))
    over = total[:, band:]
    steps = [(i, i + 1) for i in range(peers - 1)]
    swap = [(i, i ^ 1) for i in range(peers)]
    plane = mine + lax.ppermute(other, "dev", swap)
    incoming = lax.ppermute(over, "dev", steps)
    parts = exchanged(plane.reshape(16, size // 16, size), WIDE)
    share = jnp.sum(parts, axis=0)
    share = jnp.sum(copies(share, LINE), axis=0)
    share, total = lax.optimization_barrier((share, total))
    own = total[:, :band]
    new_field = object_field - jnp.concatenate(
        [own[:, :size] + incoming, own[:, size:]], axis=1
    ) * scale[None]
    plane = copies(share, WIDE).reshape(size, size)
    plane, new_field = lax.optimization_barrier((plane, new_field))
    plane_other = lax.ppermute(plane, "dev", swap)

    new_probe = pl.pallas_call(
        update_kernel,
        out_shape=jax.ShapeDtypeStruct(probe.shape, f32),
        in_specs=[smem, vmem, vmem, vmem],
        out_specs=hbm,
        scratch_shapes=[pltpu.VMEM(probe.shape, f32), pltpu.SemaphoreType.DMA((4,))],
        compiler_params=pltpu.CompilerParams(vmem_limit_bytes=8 * 1024 * 1024),
        cost_estimate=pl.CostEstimate(flops=1_000_000, bytes_accessed=1_600_000, transcendentals=1),
        name="update",
    )(facts, plane, plane_other, probe)
    return (new_field, new_probe)


def solution(mesh):
    return jax.shard_map(
        on_device,
        mesh=mesh,
        in_specs=(
            P(None, ("region", "dev"), None),
            P(),
            P("region", "dev", None, None, None),
            P("region", "dev", None),
            P("region", "dev", None),
            P("region", "dev"),
        ),
        out_specs=(P(None, ("region", "dev"), None), P()),
        check_vma=False,
    )
```

```python
import numpy as np
import ml_dtypes

import jax
import jax.numpy as jnp
from jax import lax
from jax.experimental import pallas as pl
from jax.experimental.pallas import tpu as pltpu
from jax.sharding import PartitionSpec as P

AXES = ("region", "dev")
SLOTS = 4
COUNT, CORE = 2 * SLOTS, 2 * SLOTS + 1
BLOCK = 32
WIDE = (("x_lo", "z"), ("x_lo", "y"))
LINE = (("x_hi", "y"), ("x_hi", "z"))


def in_two(table):
    high = table.astype(ml_dtypes.bfloat16)
    low = (table - high.astype(np.float64)).astype(ml_dtypes.bfloat16)
    return high, low


def half_tables(length):
    half = length // 2
    k = np.arange(half)[:, None]
    n = np.arange(half)[None, :]
    forms = []
    for shift in (0, 1):
        turn = (n * (2 * k + shift)) % length
        angle = -2.0 * np.pi * turn / length
        real = np.cos(angle) / np.sqrt(length)
        imag = np.sin(angle) / np.sqrt(length)
        forms.append(np.block([[real, -imag], [imag, real]]))
    return forms


def frame_tables(length):
    first, second = half_tables(length)
    parts = [in_two(form) for form in (first, first.T, second, second.T)]
    return np.stack([np.stack(pair) for pair in parts])


def order_table(length):
    half = length // 2
    table = np.zeros((length, length), np.float32)
    table[2 * np.arange(half), np.arange(half)] = 1.0
    table[2 * np.arange(half) + 1, half + np.arange(half)] = 1.0
    return table.astype(ml_dtypes.bfloat16)


def split2(x):
    high = x.astype(jnp.bfloat16)
    low = (x - high.astype(jnp.float32)).astype(jnp.bfloat16)
    return high, low


def placed(row, col):
    block = jnp.minimum(col // 128, 1)
    return (
        pl.multiple_of(row // 8 * 8, 8),
        row % 8,
        pl.multiple_of(block * 128, 128),
        col - block * 128,
    )


def corner(facts, source, frame):
    return facts[source, frame], facts[source, SLOTS + frame]


def tiles(x):
    return x.reshape(x.shape[0] // 8, 8, x.shape[1])


def cut_columns(x, rest):
    shift = (128 - rest) & 127
    r = [pltpu.roll(x[:, 128 * j : 128 * j + 128], shift, axis=1) for j in range(3)]
    inside = lax.broadcasted_iota(jnp.int32, r[0].shape, 1) < 128 - rest
    return jnp.concatenate([jnp.where(inside, r[0], r[1]), jnp.where(inside, r[1], r[2])], axis=1)


def turned(x, shift):
    return pltpu.roll(tiles(x), shift & 7, axis=1)


def read_window(read, size, rest_row, rest_col, use):
    after = turned(cut_columns(read(size, 8), rest_col), 8 - rest_row)
    for i in reversed(range(size // BLOCK)):
        here = turned(cut_columns(read(i * BLOCK, BLOCK), rest_col), 8 - rest_row)
        later = jnp.concatenate([here[1:], after], axis=0)
        sub = lax.broadcasted_iota(jnp.int32, here.shape, 1)
        use(i, jnp.where(sub < 8 - rest_row, here, later).reshape(BLOCK, -1))
        after = here[:1]


def moved_columns(x, rest):
    shift = rest & 127
    ra = pltpu.roll(x[:, :128], shift, axis=1)
    rb = pltpu.roll(x[:, 128:], shift, axis=1)
    inside = lax.broadcasted_iota(jnp.int32, ra.shape, 1) >= rest
    zero = jnp.zeros_like(ra)
    return jnp.concatenate(
        [jnp.where(inside, ra, zero), jnp.where(inside, rb, ra), jnp.where(inside, zero, rb)], axis=1
    )


def moved_rows(x, before, rest_row):
    here = turned(x, rest_row)
    earlier = jnp.concatenate([before, here[:-1]], axis=0)
    sub = lax.broadcasted_iota(jnp.int32, here.shape, 1)
    return jnp.where(sub >= rest_row, here, earlier).reshape(x.shape), here[-1:]


def last_rows(before, rest_row):
    sub = lax.broadcasted_iota(jnp.int32, before.shape, 1)
    return jnp.where(sub >= rest_row, 0.0, before).reshape(8, -1)


def prepare_kernel(facts, amp_ref, probe_ref, order_ref, out_ref, weight_ref, total, side):
    band = weight_ref.shape[0]
    size = probe_ref.shape[1]
    half = size // 2
    total[...] = jnp.zeros_like(total)

    def add_power(source, frame, down):
        start, rest_row, base, rest_col = placed(*corner(facts, source, frame))
        before = jnp.zeros((1, 8, 384), jnp.float32)
        for i in range(size // BLOCK):
            pr = probe_ref[0, i * BLOCK : (i + 1) * BLOCK, :]
            pi = probe_ref[1, i * BLOCK : (i + 1) * BLOCK, :]
            part, before = moved_rows(moved_columns(pr * pr + pi * pi, rest_col), before, rest_row)
            place = (pl.ds(start + (down + i * BLOCK), BLOCK), pl.ds(base, 384))
            total[place] = total[place] + part
        place = (pl.ds(start + (down + size), 8), pl.ds(base, 384))
        total[place] = total[place] + last_rows(before, rest_row)

    def own(frame, carry):
        add_power(0, frame, band)
        return carry

    def previous(frame, carry):
        add_power(1, frame, 0)
        return carry

    lax.fori_loop(0, facts[0, COUNT], own, 0)
    lax.fori_loop(0, facts[1, COUNT], previous, 0)
    for i in range(band // BLOCK):
        weight_ref[i * BLOCK : (i + 1) * BLOCK, :] = 1.0 / (
            total[band + i * BLOCK : band + (i + 1) * BLOCK, :] + 1.0
        )

    def permute(frame, carry):
        x = amp_ref[frame]
        high = x.astype(jnp.bfloat16)
        left = x - high.astype(jnp.float32)
        mid = left.astype(jnp.bfloat16)
        low = (left - mid.astype(jnp.float32)).astype(jnp.bfloat16)
        order = order_ref[...]
        y = (
            jnp.dot(high, order, preferred_element_type=jnp.float32)
            + jnp.dot(mid, order, preferred_element_type=jnp.float32)
            + jnp.dot(low, order, preferred_element_type=jnp.float32)
        )
        for j in (0, 1):
            column = slice(j * half, (j + 1) * half)
            side[...] = y[:, column]
            for parity in (0, 1):
                out_ref[frame, parity * half : (parity + 1) * half, column] = side[
                    pl.ds(parity, half, stride=2), :
                ]
        return carry

    lax.fori_loop(0, facts[0, COUNT], permute, 0)


def frames_kernel(
    facts, ext, probe, amp, tables,
    mine_ref, other_ref, total,
    win, xh, xl, fa, fb, grad,
):
    size = probe.shape[1]
    half = size // 2
    steps = half // BLOCK
    count = facts[0, COUNT]

    total[...] = jnp.zeros_like(total)
    grad[...] = jnp.zeros_like(grad)

    def keep(b, which, place, value):
        high, low = split2(value)
        xh[(b, which, *place)] = high
        xl[(b, which, *place)] = low

    def by_right(b, which, table):
        high = xh[b, which]
        x = jnp.concatenate([high, xl[b, which], high], axis=1)
        t = tables[table, 0]
        t = jnp.concatenate([t, t, tables[table, 1]], axis=0)
        return jnp.dot(x, t, preferred_element_type=jnp.float32)

    def by_left(b, which, table):
        high = xh[b, which]
        x = jnp.concatenate([high, xl[b, which], high], axis=0)
        t = tables[table, 0]
        t = jnp.concatenate([t, t, tables[table, 1]], axis=1)
        return jnp.dot(t, x, preferred_element_type=jnp.float32)

    def cut(b, place):
        start, rest_row, base, rest_col = place

        def into(c):
            def use(i, rows_cut):
                win[b, c, i * BLOCK : (i + 1) * BLOCK, :] = rows_cut

            return use

        for c in (0, 1):
            read_window(
                lambda at, rows: ext[c, pl.ds(start + at, rows), pl.ds(base, 384)],
                size, rest_row, rest_col, into(c),
            )
        for i in range(size // BLOCK):
            row = slice(i * BLOCK, (i + 1) * BLOCK)
            wr, wi = win[b, 0, row, :], win[b, 1, row, :]
            pr, pi = probe[0, row, :], probe[1, row, :]
            er = pr * wr - pi * wi
            ei = pr * wi + pi * wr
            keep(b, 0, (row, slice(0, half)), er[:, :half] + er[:, half:])
            keep(b, 0, (row, slice(half, size)), ei[:, :half] + ei[:, half:])
            keep(b, 1, (row, slice(0, half)), er[:, :half] - er[:, half:])
            keep(b, 1, (row, slice(half, size)), ei[:, :half] - ei[:, half:])

    def right_forward(b):
        fa[b] = by_right(b, 0, 1)
        fb[b] = by_right(b, 1, 3)

    def fold_rows(b):
        for i in range(steps):
            top = slice(i * BLOCK, (i + 1) * BLOCK)
            low = slice(half + i * BLOCK, half + (i + 1) * BLOCK)
            for ref, out in ((fa, slice(0, half)), (fb, slice(half, size))):
                t, u = ref[b, top, :], ref[b, low, :]
                s, d = t + u, t - u
                keep(b, 0, (top, out), s[:, :half])
                keep(b, 0, (low, out), s[:, half:])
                keep(b, 1, (top, out), d[:, :half])
                keep(b, 1, (low, out), d[:, half:])

    def left_forward(b):
        fa[b] = by_left(b, 0, 0)
        fb[b] = by_left(b, 1, 2)

    def correct(b, frame, live):
        for i in range(steps):
            top = slice(i * BLOCK, (i + 1) * BLOCK)
            low = slice(half + i * BLOCK, half + (i + 1) * BLOCK)
            for which, ref in ((0, fa), (1, fb)):
                re, im = ref[b, top, :], ref[b, low, :]
                a = amp[frame, pl.ds(which * half + i * BLOCK, BLOCK), :]
                factor = 1.0 - a * lax.rsqrt(re * re + im * im + 0.25)
                factor = jnp.where(live, factor, 0.0)
                keep(b, which, (top, slice(0, size)), re * factor)
                keep(b, which, (low, slice(0, size)), im * factor)

    def left_back(b):
        fa[b] = by_left(b, 0, 1)
        fb[b] = by_left(b, 1, 3)

    def unfold_rows(b):
        for i in range(steps):
            top = slice(i * BLOCK, (i + 1) * BLOCK)
            low = slice(half + i * BLOCK, half + (i + 1) * BLOCK)
            for part, out in ((top, slice(0, half)), (low, slice(half, size))):
                p, q = fa[b, part, :], fb[b, part, :]
                s, d = p + q, p - q
                for place, v in ((top, s), (low, d)):
                    keep(b, 0, (place, out), v[:, :half])
                    keep(b, 1, (place, out), v[:, half:])

    def right_back(b):
        fa[b] = by_right(b, 0, 0)
        fb[b] = by_right(b, 1, 2)

    def spread(b, place):
        start, rest_row, base, rest_col = place
        before = [jnp.zeros((1, 8, 384), jnp.float32)] * 2
        for i in range(size // BLOCK):
            row = slice(i * BLOCK, (i + 1) * BLOCK)
            p, q = fa[b, row, :], fb[b, row, :]
            s, d = p + q, p - q
            br = jnp.concatenate([s[:, :half], d[:, :half]], axis=1)
            bi = jnp.concatenate([s[:, half:], d[:, half:]], axis=1)
            wr, wi = win[b, 0, row, :], win[b, 1, row, :]
            grad[0, row, :] = grad[0, row, :] + (wr * br + wi * bi)
            grad[1, row, :] = grad[1, row, :] + (wr * bi - wi * br)
            pr, pi = probe[0, row, :], probe[1, row, :]
            for c, v in ((0, pr * br + pi * bi), (1, pr * bi - pi * br)):
                part, before[c] = moved_rows(moved_columns(v, rest_col), before[c], rest_row)
                at = (c, pl.ds(start + i * BLOCK, BLOCK), pl.ds(base, 384))
                total[at] = total[at] + part
        for c in (0, 1):
            at = (c, pl.ds(start + size, 8), pl.ds(base, 384))
            total[at] = total[at] + last_rows(before[c], rest_row)

    def two_frames(pair, carry):
        frames = (2 * pair, 2 * pair + 1)
        places = [placed(*corner(facts, 0, frame)) for frame in frames]
        both = (0, 1)
        cut(0, places[0])
        right_forward(0)
        cut(1, places[1])
        right_forward(1)
        for elementwise, product in (
            (lambda b: fold_rows(b), left_forward),
            (lambda b: correct(b, frames[b], frames[b] < count), left_back),
            (lambda b: unfold_rows(b), right_back),
        ):
            for b in both:
                elementwise(b)
                product(b)
        for b in both:
            spread(b, places[b])
        return carry

    lax.fori_loop(0, (count + 1) // 2, two_frames, 0)
    first = facts[0, CORE] == 0
    for i in range(size // BLOCK):
        row = slice(i * BLOCK, (i + 1) * BLOCK)
        re, im = grad[0, row, :], grad[1, row, :]
        mine_ref[row, :] = jnp.where(first, re, im)
        other_ref[row, :] = jnp.where(first, im, re)


def update_kernel(facts, mine_ref, other_ref, probe_ref, out_ref, held, sems):
    size = mine_ref.shape[0]
    total = jnp.zeros((8, size), jnp.float32)
    for i in range(size // 8):
        row = slice(8 * i, 8 * i + 8)
        mine, other = mine_ref[row, :], other_ref[row, :]
        total = total + (mine * mine + other * other)
    squares = jnp.sum(total)
    step = 0.25 * lax.rsqrt(jnp.full((1, 1), squares / (2 * size * size) + 1e-06, jnp.float32))
    first = facts[0, CORE] == 0
    stores = []
    for j in range(2):
        row = slice(j * size // 2, (j + 1) * size // 2)
        mine, other = mine_ref[row, :], other_ref[row, :]
        for c, part in ((0, jnp.where(first, mine, other)), (1, jnp.where(first, other, mine))):
            held[c, row, :] = probe_ref[c, row, :] - step * part
            stores.append(
                pltpu.make_async_copy(held.at[c, row], out_ref.at[c, row], sems.at[2 * j + c])
            )
            stores[-1].start()
    for store in stores:
        store.wait()


def place_of(device):
    region, dev = divmod(device, 64)
    return {
        "x_hi": region // 4,
        "x_lo": region // 2 % 2,
        "z": (region % 2) * 4 + (dev // 2) % 4,
        "y": dev // 8,
        "core": dev % 2,
    }


def groups_along(by_core):
    groups = {}
    for device in range(512):
        place = place_of(device)
        key = tuple(v for k, v in place.items() if k not in by_core[place["core"]])
        groups.setdefault((place["core"], key), []).append(device)
    return list(groups.values())


def exchanged(parts, names):
    return lax.all_to_all(parts, AXES, 0, 0, tiled=True, axis_index_groups=groups_along(names))


def copies(part, names):
    peers = len(groups_along(names)[0])
    return exchanged(jnp.broadcast_to(part[None], (peers, *part.shape)), names)


def on_device(object_field, probe, amplitudes, row_offset, col_offset, frame_count):
    band, width = object_field.shape[1:]
    size = probe.shape[1]
    slots = amplitudes.shape[2]
    smem = pl.BlockSpec(memory_space=pltpu.SMEM)
    vmem = pl.BlockSpec(memory_space=pltpu.VMEM)
    hbm = pl.BlockSpec(memory_space=pltpu.HBM)
    f32 = jnp.float32
    peers = lax.axis_size("dev")

    rim = lax.ppermute(object_field, "dev", [(i, i - 1) for i in range(1, peers)])
    core = (lax.axis_index("dev") % 2).astype(jnp.int32)
    facts = jnp.concatenate([row_offset[0, 0], col_offset[0, 0], frame_count[0], core[None]])
    facts_before = lax.ppermute(facts, "dev", [(i, i + 1) for i in range(peers - 1)])
    facts = jnp.stack([facts, facts_before])

    ordered, scale = pl.pallas_call(
        prepare_kernel,
        out_shape=(
            jax.ShapeDtypeStruct((slots, size, size), f32),
            jax.ShapeDtypeStruct((band, width), f32),
        ),
        in_specs=[smem, vmem, vmem, vmem],
        out_specs=(vmem, vmem),
        scratch_shapes=[
            pltpu.VMEM((2 * band + size, width), f32),
            pltpu.VMEM((size, size // 2), f32),
        ],
        compiler_params=pltpu.CompilerParams(vmem_limit_bytes=24000 * 1024),
        cost_estimate=pl.CostEstimate(flops=800_000_000, bytes_accessed=3_200_000, transcendentals=0),
        name="prepare",
    )(facts, amplitudes[0, 0], probe, jnp.asarray(order_table(size)))

    bf16 = jnp.bfloat16
    ext = jnp.pad(object_field, ((0, 0), (0, size), (0, 0)))
    ext, rim = lax.optimization_barrier((ext, rim))
    ext = lax.dynamic_update_slice(ext, rim[:, :size], (0, band, 0))
    mine, other, total = pl.pallas_call(
        frames_kernel,
        out_shape=(
            jax.ShapeDtypeStruct((size, size), f32),
            jax.ShapeDtypeStruct((size, size), f32),
            jax.ShapeDtypeStruct((2, band + size, width), f32),
        ),
        in_specs=[smem, vmem, vmem, vmem, vmem],
        out_specs=(vmem, vmem, vmem),
        scratch_shapes=[
            pltpu.VMEM((2, 2, size, size), f32),
            pltpu.VMEM((2, 2, size, size), bf16),
            pltpu.VMEM((2, 2, size, size), bf16),
            pltpu.VMEM((2, size, size), f32),
            pltpu.VMEM((2, size, size), f32),
            pltpu.VMEM((2, size, size), f32),
        ],
        compiler_params=pltpu.CompilerParams(vmem_limit_bytes=24 * 1024 * 1024),
        cost_estimate=pl.CostEstimate(flops=3_300_000_000, bytes_accessed=8_000_000, transcendentals=262144),
        name="frames",
    )(facts, ext, probe, ordered, jnp.asarray(frame_tables(size)))
    steps = [(i, i + 1) for i in range(peers - 1)]
    swap = [(i, i ^ 1) for i in range(peers)]
    plane = mine + lax.ppermute(other, "dev", swap)
    parts = exchanged(plane.reshape(16, size // 16, size), WIDE)
    share = jnp.sum(parts, axis=0)
    share, total = lax.optimization_barrier((share, total))
    incoming = lax.ppermute(total[:, band:], "dev", steps)
    share = jnp.sum(copies(share, LINE), axis=0)
    share, total = lax.optimization_barrier((share, total))
    own = total[:, :band]
    new_field = object_field - jnp.concatenate(
        [own[:, :size] + incoming, own[:, size:]], axis=1
    ) * scale[None]
    plane = copies(share, WIDE).reshape(size, size)
    plane, new_field = lax.optimization_barrier((plane, new_field))
    plane_other = lax.ppermute(plane, "dev", swap)

    new_probe = pl.pallas_call(
        update_kernel,
        out_shape=jax.ShapeDtypeStruct(probe.shape, f32),
        in_specs=[smem, vmem, vmem, vmem],
        out_specs=hbm,
        scratch_shapes=[pltpu.VMEM(probe.shape, f32), pltpu.SemaphoreType.DMA((4,))],
        compiler_params=pltpu.CompilerParams(vmem_limit_bytes=8 * 1024 * 1024),
        cost_estimate=pl.CostEstimate(flops=1_000_000, bytes_accessed=1_600_000, transcendentals=1),
        name="update",
    )(facts, plane, plane_other, probe)
    return (new_field, new_probe)


def solution(mesh):
    return jax.shard_map(
        on_device,
        mesh=mesh,
        in_specs=(
            P(None, ("region", "dev"), None),
            P(),
            P("region", "dev", None, None, None),
            P("region", "dev", None),
            P("region", "dev", None),
            P("region", "dev"),
        ),
        out_specs=(P(None, ("region", "dev"), None), P()),
        check_vma=False,
    )
```
